32 devices in a mesh: leaf: 8 (over z, y), bond: 4 (over x, core).
Axes of the slice: x: 2, y: 2, z: 4, core: 2. Of those that a mesh axis runs over, the one named last changes fastest.
Arguments:
- leaf_metric: float32 [4, 32, 1024], P('bond', 'leaf'), may hold values from -257 to 257, as said below
- local_iso: float32 [24, 32, 1024], P('leaf', 'bond'), may hold values from -6 to 6
- top_iso: float32 [8, 32, 1024], P('leaf', 'bond'), may hold values from -6 to 6
Outputs:
- leaf_rho: float32 [4, 32, 1024], P('bond', 'leaf')
- inner_rho: float32 [4, 24, 1024], P('bond', 'leaf')
- top_rho: float32 [4, 8, 1024], P('bond', 'leaf')
The draws below stay inside these ranges and needn't reach their ends.
Inputs may be any that keep to these rules, and one draw needn't show every extreme that they name: Each entry of leaf_metric, taken as a 32 x 32 matrix, is symmetric positive definite.
All inputs are finite; a program needn't handle non-finite values.
Results may differ from the reference program's by a relative error of at most 0.0003.
Values sent between devices are 32-bit elements; how exact they have to be, the bound alone decides.
A program may use at most 64 MiB of HBM per device.

```python
import math
import jax
import jax.numpy as jnp
from jax import lax

CHI = 32
LEAVES_DEV = 4
CHI2 = 1024
LEAVES = 32
INNER = 24
BATCH = 4
N_LEAF = 8


def draw_leaf_metric(key, part):
    first_key, second_key = jax.random.split(key)
    base = jax.random.truncated_normal(first_key, -4.0, 4.0, (BATCH, LEAVES, CHI, CHI), jnp.float32)
    spread = jax.random.uniform(second_key, (BATCH, LEAVES, CHI), jnp.float32, math.log(0.4), math.log(2.5))
    rows = base * jnp.exp(spread)[..., None]
    metric = jnp.einsum('mlac,mlbc->mlab', rows, rows) / CHI + 0.5 * jnp.eye(CHI, dtype=jnp.float32)
    return metric.reshape(BATCH, LEAVES, CHI2)


def isometry_law(key, node_rows):
    keys = jax.random.split(key, 4)
    left_gain = jax.random.truncated_normal(keys[0], -4.0, 4.0, (node_rows, CHI), jnp.float32) / math.sqrt(CHI)
    right_gain = jax.random.truncated_normal(keys[1], -4.0, 4.0, (node_rows, CHI), jnp.float32) / math.sqrt(CHI)
    identity = jnp.eye(CHI, dtype=jnp.float32)
    structured = identity[None, :, :, None] * left_gain[:, None, None, :] + identity[None, :, None, :] * right_gain[:, None, :, None]
    noise = jax.random.truncated_normal(keys[2], -4.0, 4.0, (node_rows, CHI, CHI, CHI), jnp.float32) / CHI
    parent_scale = jnp.exp(jax.random.uniform(keys[3], (node_rows, CHI), jnp.float32, math.log(0.5), math.log(2.0)))
    return ((structured + noise) * parent_scale[:, :, None, None]).reshape(node_rows, CHI, CHI2)


def draw_local_iso(key, part):
    return isometry_law(jax.random.fold_in(key, 11), INNER)


def draw_top_iso(key, part):
    base_key = jax.random.fold_in(key, 23)
    levels = N_LEAF.bit_length() - 1
    blocks = []
    for height in range(1, levels + 1):
        groups = N_LEAF >> height
        logical = isometry_law(jax.random.fold_in(base_key, height), groups)
        width = CHI2 >> height
        shares = jnp.transpose(logical.reshape(groups, CHI, 2 ** height, width), (0, 2, 1, 3))
        blocks.append(shares.reshape(N_LEAF, CHI, width))
    root_tensor = isometry_law(jax.random.fold_in(base_key, 99), 1)
    width = CHI2 >> levels
    blocks.append(jnp.transpose(root_tensor.reshape(CHI, N_LEAF, width), (1, 0, 2)))
    return jnp.concatenate(blocks, axis=2)


def setup_inputs(seed: int = 0) -> dict:
    streams_of = jax.random.split(jax.random.key(seed), 4)
    return {
        "leaf_metric": draw_leaf_metric(jax.random.fold_in(streams_of[3], 71), 0),
        "local_iso": draw_local_iso(jax.random.fold_in(streams_of[3], 71), 0),
        "top_iso": draw_top_iso(jax.random.fold_in(streams_of[3], 71), 0),
    }


exact_mode = lax.Precision.HIGHEST


def normalize(matrix):
    trace_value = jnp.trace(matrix, axis1=-2, axis2=-1)
    return matrix * (CHI / trace_value)[..., None, None]


def grow(tensor, left_env, right_env):
    first = jnp.einsum('npab,mnac->mnpcb', tensor, left_env, precision=exact_mode)
    second = jnp.einsum('mnpcb,mnbd->mnpcd', first, right_env, precision=exact_mode)
    third = jnp.einsum('mnpcd,nqcd->mnpq', second, tensor, precision=exact_mode)
    return normalize(third)


def descend(tensor, parent_state, left_env, right_env):
    mixed = jnp.einsum('mnpq,npab->mnqab', parent_state, tensor, precision=exact_mode)
    left_part = jnp.einsum('mnqab,mnbd->mnqad', mixed, right_env, precision=exact_mode)
    left_state = jnp.einsum('mnqad,nqcd->mnac', left_part, tensor, precision=exact_mode)
    right_part = jnp.einsum('mnqab,mnac->mnqcb', mixed, left_env, precision=exact_mode)
    right_state = jnp.einsum('mnqcb,nqcd->mnbd', right_part, tensor, precision=exact_mode)
    return normalize(left_state), normalize(right_state)


def blockwise(function, tensor, *matrices):
    node_total = tensor.shape[0]
    per_block = min(node_total, 16)
    groups = node_total // per_block
    grouped_tensor = tensor.reshape((groups, per_block) + tensor.shape[1:])
    grouped = [jnp.moveaxis(item.reshape((item.shape[0], groups, per_block) + item.shape[2:]), 1, 0) for item in matrices]

    def apply_block(operands):
        return function(operands[0], *operands[1:])

    result = lax.map(apply_block, tuple([grouped_tensor] + grouped))

    def restore(item):
        moved = jnp.moveaxis(item, 0, 1)
        return moved.reshape((moved.shape[0], node_total) + moved.shape[3:])

    return jax.tree.map(restore, result)


def unpack_level(top_iso, height):
    width = CHI2 >> height
    start = CHI2 - (CHI2 >> (height - 1))
    block = top_iso[:, :, start:start + width]
    groups = N_LEAF >> height
    block = block.reshape(groups, 2 ** height, CHI, width)
    return jnp.transpose(block, (0, 2, 1, 3)).reshape(groups, CHI, CHI, CHI)


def unpack_root(top_iso, levels):
    width = CHI2 >> levels
    block = top_iso[:, :, CHI2 - width:]
    return jnp.transpose(block, (1, 0, 2)).reshape(CHI, CHI, CHI)


def reference(leaf_metric, local_iso, top_iso):
    levels_dev = LEAVES_DEV.bit_length() - 1
    top_levels = N_LEAF.bit_length() - 1
    leaves = leaf_metric.reshape(BATCH, LEAVES, CHI, CHI)
    local_all = local_iso.reshape(N_LEAF, LEAVES_DEV - 1, CHI, CHI, CHI)
    tensors = []
    for height in range(1, levels_dev + 1):
        node_count = LEAVES_DEV >> height
        offset = LEAVES_DEV - 2 * node_count
        tensors.append(local_all[:, offset:offset + node_count].reshape(-1, CHI, CHI, CHI))
    for height in range(1, top_levels + 1):
        tensors.append(unpack_level(top_iso, height))
    envs = [leaves]
    for tensor in tensors:
        current = envs[-1]
        envs.append(blockwise(grow, tensor, current[:, 0::2], current[:, 1::2]))
    root_env = envs[-1][:, 0]
    root_tensor = unpack_root(top_iso, top_levels)
    gram = jnp.einsum('pab,qab->pq', root_tensor, root_tensor, precision=exact_mode)
    state = jnp.broadcast_to(normalize(gram), (BATCH, 1, CHI, CHI))
    total = len(tensors)
    collected = [state] * (total + 1)
    for level_index in range(total - 1, -1, -1):
        children = envs[level_index]
        left_state, right_state = blockwise(descend, tensors[level_index], state, children[:, 0::2], children[:, 1::2])
        state = jnp.stack([left_state, right_state], axis=2).reshape(BATCH, -1, CHI, CHI)
        collected[level_index] = state
    top = jnp.zeros((BATCH, N_LEAF, CHI, CHI), jnp.float32)
    for height in range(1, top_levels + 1):
        top = top.at[:, 2 ** (height - 1) - 1::2 ** height].set(collected[levels_dev + height])
    top = top.at[:, N_LEAF - 1].set(root_env)
    inner = jnp.zeros((BATCH, N_LEAF, LEAVES_DEV - 1, CHI, CHI), jnp.float32)
    for height in range(1, levels_dev + 1):
        node_count = LEAVES_DEV >> height
        offset = LEAVES_DEV - 2 * node_count
        inner = inner.at[:, :, offset:offset + node_count].set(collected[height].reshape(BATCH, N_LEAF, node_count, CHI, CHI))
    leaf_rho = collected[0].reshape(BATCH, LEAVES, CHI2)
    inner_rho = inner.reshape(BATCH, INNER, CHI2)
    top_rho = top.reshape(BATCH, N_LEAF, CHI2)
    return (leaf_rho, inner_rho, top_rho)
```

```python
import functools

import jax
import jax.numpy as jnp
from jax import lax
from jax.experimental import pallas as pl
from jax.experimental.pallas import tpu as pltpu
from jax.sharding import PartitionSpec as P

LANES = 128
MESH = pl.DeviceIdType.MESH
EXACT = lax.Precision.HIGHEST
JOINT = 2


def mm(a, b):
    return jnp.dot(a, b, precision=EXACT, preferred_element_type=jnp.float32)


def dot(a, b):
    return jnp.dot(a, b, preferred_element_type=jnp.float32)


def dot_nt(a, b):
    return lax.dot_general(a, b, (((1,), (1,)), ((), ())), preferred_element_type=jnp.float32)


def halves(value):
    high = value.astype(jnp.bfloat16)
    low = (value - high.astype(jnp.float32)).astype(jnp.bfloat16)
    return high, low


def join_lanes(value):
    return value[:, :LANES] + value[:, LANES:]


def join_rows(value):
    half = value.shape[0] // 2
    return value[:half] + value[half:]


def kernel(
    cfg,
    leaf_hbm,
    local_hbm,
    top_hbm,
    out,
    leaf_ref,
    raw,
    loc,
    wk,
    wm,
    wq,
    yt,
    fbuf,
    perm,
    esend,
    erecv,
    own_sem,
    loc_send,
    loc_recv,
    leaf_send,
    leaf_recv,
    fwd_send,
    fwd_recv,
    env_send,
    env_recv,
):
    chi, leaves, devices, bonds = cfg
    cols = chi * chi
    rep = LANES // chi
    chunks = cols // LANES
    levels = devices.bit_length() - 1
    height_dev = leaves.bit_length() - 1
    nodes = leaves - 1
    joint = min(JOINT, levels)
    span = 1 << joint
    position = lax.axis_index("leaf")
    mine = lax.axis_index("bond")

    hops = list(range(1, span)) + [1 << k for k in range(joint, levels)]
    bits = [1 << b for b in reversed(range(bonds.bit_length() - 1))]

    barrier = pltpu.get_barrier_semaphore()
    for hop in hops:
        pl.semaphore_signal(barrier, inc=1, device_id=(position ^ hop, mine), device_id_type=MESH)
    for bit in bits:
        pl.semaphore_signal(barrier, inc=1, device_id=(position, mine ^ bit), device_id_type=MESH)
    own = [
        pltpu.make_async_copy(local_hbm, loc.at[mine], own_sem.at[0]),
        pltpu.make_async_copy(top_hbm.at[0], raw.at[mine, position], own_sem.at[1]),
        pltpu.make_async_copy(leaf_hbm, leaf_ref, own_sem.at[2]),
    ]
    for copy in own:
        copy.start()
    own[0].wait()
    own[1].wait()
    pl.semaphore_wait(barrier, len(hops) + len(bits))

    starts = [cols - (cols >> k) for k in range(levels + 1)]
    aligned = [s // LANES * LANES for s in starts]
    stops = [-(-s // LANES) * LANES for s in starts[1:-1]] + [cols]
    sends = []

    class Spread:
        def __init__(self, slices, send_sem, recv_sem):
            self.copies = {}
            self.left = set(range(1, bonds))
            for d in range(1, bonds):
                bit = d & -d
                ref = slices(mine ^ (d ^ bit))
                self.copies[d] = pltpu.make_async_remote_copy(
                    src_ref=ref,
                    dst_ref=ref,
                    send_sem=send_sem.at[d - 1],
                    recv_sem=recv_sem.at[d - 1],
                    device_id=(position, mine ^ bit),
                    device_id_type=MESH,
                )

        def start(self):
            for bit in bits:
                self.copies[bit].start()
                sends.append(self.copies[bit])
            return self

        def recv(self, d):
            if d in self.left:
                self.left.remove(d)
                self.copies[d].wait_recv()

        def forward(self):
            for bit in bits:
                for d in range(1, bonds):
                    if d & -d == bit and d != bit:
                        self.recv(d ^ bit)
                        self.copies[d].start()
                        sends.append(self.copies[d])

        def finish(self):
            for d in sorted(self.left):
                self.recv(d)

    def leaf_copy(n, hop, slots):
        copy = pltpu.make_async_remote_copy(
            src_ref=slots,
            dst_ref=slots,
            send_sem=leaf_send.at[n],
            recv_sem=leaf_recv.at[n],
            device_id=(position ^ hop, mine),
            device_id_type=MESH,
        )
        copy.start()
        sends.append(copy)
        return copy

    def block(level):
        return (position >> level) << level

    local_moves = []
    for n in range(nodes):
        local_moves.append(
            Spread(lambda j, n=n: loc.at[j, n], loc_send.at[n], loc_recv.at[n]).start()
        )
    group_moves = [
        leaf_copy(hop - 1, hop, raw.at[mine, position]) for hop in reversed(range(1, span))
    ]
    far_moves = []
    top_moves = []

    def far_copy(k):
        slots = raw.at[mine, pl.ds(block(k), 1 << k), :, aligned[k] : cols]
        far_moves.append(leaf_copy(span - 1 + k - joint, 1 << k, slots))

    def top_spread(k):
        if k < joint:
            base, count, lo, hi = block(joint), span, 0, stops[joint - 1]
        else:
            base, count, lo, hi = block(k + 1), 2 << k, aligned[k], stops[k]
        n = len(top_moves)
        top_moves.append(
            Spread(
                lambda j: raw.at[j, pl.ds(base, count), :, lo:hi], fwd_send.at[n], fwd_recv.at[n]
            ).start()
        )

    own[2].wait()

    row = lax.broadcasted_iota(jnp.int32, (chi, LANES), 0)
    lane = lax.broadcasted_iota(jnp.int32, (chi, LANES), 1)
    group = lane // chi
    row_mask = group == lax.rem(row, rep)
    diag_mask = row == lane
    big_row = lax.broadcasted_iota(jnp.int32, (LANES, LANES), 0)
    big_lane = lax.broadcasted_iota(jnp.int32, (LANES, LANES), 1)
    block_mask = big_row // chi == big_lane // chi
    pick = (
        lax.broadcasted_iota(jnp.int32, (chunks, chi), 1) // rep
        == lax.broadcasted_iota(jnp.int32, (chunks, chi), 0)
    ).astype(jnp.float32)
    spread = (
        lax.broadcasted_iota(jnp.int32, (chi, chunks), 0) // rep
        == lax.broadcasted_iota(jnp.int32, (chi, chunks), 1)
    ).astype(jnp.float32)
    sub = chi // rep
    widen = (
        lax.broadcasted_iota(jnp.int32, (LANES, chi * sub), 1) // sub
        == lax.rem(lax.broadcasted_iota(jnp.int32, (LANES, chi * sub), 0), chi)
    ).astype(jnp.float32).astype(jnp.bfloat16)
    unit_mask = lax.rem(
        lax.broadcasted_iota(jnp.int32, (sub, chi * sub), 1), sub
    ) == lax.broadcasted_iota(jnp.int32, (sub, chi * sub), 0)
    column = lax.broadcasted_iota(jnp.int32, (chi, cols), 1)
    swapped_column = lax.broadcasted_iota(jnp.int32, (chi, cols), 0) * chi

    @pl.loop(0, chi)
    def _(a):
        perm[pl.ds(pl.multiple_of(a * chi, chi), chi), :] = (
            (column == swapped_column + a).astype(jnp.float32).astype(jnp.bfloat16)
        )

    part_group = lax.broadcasted_iota(jnp.int32, (chunks * sub, LANES), 1) // chi

    def swap_groups(value):
        parts = [
            jnp.concatenate(
                [value[g * chi + v * sub : g * chi + (v + 1) * sub] for g in range(chunks)], axis=0
            )
            for v in range(rep)
        ]
        bit = 1
        while bit < rep:
            lower = lax.rem(part_group // bit, 2) == 0
            for a in range(rep):
                if a & bit == 0:
                    one, two = parts[a], parts[a | bit]
                    parts[a] = jnp.where(lower, one, pltpu.roll(two, bit * chi, 1))
                    parts[a | bit] = jnp.where(lower, pltpu.roll(one, LANES - bit * chi, 1), two)
            bit *= 2
        return jnp.concatenate(
            [parts[v][g * sub : (g + 1) * sub] for g in range(chunks) for v in range(rep)], axis=0
        )

    def fold(value):
        shift = chi
        while shift < LANES:
            value = value + pltpu.roll(value, shift, 1)
            shift *= 2
        return value

    def scaled(matrix):
        trace = jnp.sum(jnp.where(diag_mask, matrix, 0.0), axis=(0, 1), keepdims=True)
        return matrix, chi / trace

    def normal(pair):
        return pair[0] * pair[1]

    def unflatten(line):
        tile = jnp.concatenate(
            [line[:, g * LANES : (g + 1) * LANES] for g in range(chunks)], axis=0
        )
        return fold(jnp.where(row_mask, mm(spread, tile), 0.0))

    def flatten(matrix, index):
        out[index] = mm(pick, jnp.where(row_mask, matrix, 0.0))

    def lanes_to_rows(value):
        return jnp.concatenate(
            [value[:, g * LANES : (g + 1) * LANES] for g in range(chunks)], axis=0
        )

    def rows_to_lanes(value):
        return jnp.concatenate([value[g * chi : (g + 1) * chi] for g in range(chunks)], axis=1)

    def stacked(value):
        return jnp.concatenate(halves(value), axis=0)

    def permute(parts):
        stack = parts[0] if len(parts) == 1 else jnp.concatenate(parts, axis=0)
        moved = dot(stack, perm[...])
        return [join_rows(moved[n * 2 * chi : (n + 1) * 2 * chi]) for n in range(len(parts))]

    def store_down(item, value):
        high, low = halves(value)
        wm[item] = jnp.concatenate([high, low] * (rep // 2), axis=0)

    def store_up(item, value):
        high, low = halves(value)
        wk[item] = jnp.concatenate([lanes_to_rows(high), lanes_to_rows(low)], axis=1)
        wq[item] = jnp.concatenate(halves(swap_groups(lanes_to_rows(value))), axis=1)

    def keep(item, acted):
        yt[item] = stacked(acted.T)

    def act_minor(item, env):
        env, scale = env
        block = jnp.where(block_mask, jnp.concatenate([env] * rep, axis=0), 0.0)
        pair = jnp.concatenate(halves(block), axis=1)
        return rows_to_lanes(
            join_lanes(dot(wk[item], jnp.concatenate([pair, pair], axis=0))) * scale
        )

    def act_major(item, env, down=True):
        env, scale = env
        high = env.astype(jnp.bfloat16).astype(jnp.float32)
        rest = env - high
        middle = rest.astype(jnp.bfloat16).astype(jnp.float32)
        low = jnp.where(group == 2, rest - middle, 0.0)
        parts = jnp.where(group == 0, high, jnp.where(group == 1, middle, low))
        fbuf[...] = dot(parts.astype(jnp.bfloat16), widen)
        wide = jnp.concatenate(
            [
                jnp.where(unit_mask, jnp.broadcast_to(fbuf[y : y + 1, :], unit_mask.shape), 0.0)
                for y in range(chi)
            ],
            axis=0,
        )
        acted = dot(jnp.concatenate(halves(wide), axis=0), wq[item])
        acted = swap_groups(join_lanes(join_rows(acted)) * scale)
        if down:
            keep(item, acted)
        return rows_to_lanes(acted)

    def close(left, right):
        high, low = halves(right)
        wide = jnp.concatenate([high] * rep + [low] * rep, axis=0)
        tall = jnp.concatenate(halves(left), axis=0)
        return scaled(join_lanes(join_rows(dot_nt(tall, wide))))

    def descend(item, state):
        state, scale = state
        high = state.astype(jnp.bfloat16).astype(jnp.float32)
        parts = jnp.where(group < rep // 2, high, state - high).astype(jnp.bfloat16)
        mixed = lanes_to_rows(dot(parts, wm[item]) * scale)
        square = dot(yt[item], jnp.concatenate(halves(mixed), axis=1))
        square = jnp.where(block_mask, join_lanes(join_rows(square)), 0.0)
        total = square[:chi]
        for i in range(1, rep):
            total = total + square[i * chi : (i + 1) * chi]
        return scaled(fold(total))

    envs = [[(unflatten(leaf_ref[0, n : n + 1, :]), 1.0) for n in range(leaves)]]
    for move in local_moves:
        move.forward()
    for move in group_moves:
        move.wait_recv()
    if joint < levels:
        far_copy(joint)
    top_spread(0)

    late = []
    first = 0
    for height in range(1, height_dev + 1):
        current = envs[-1]
        count = leaves >> height
        for n in range(count):
            local_moves[first + n].finish()
        grown = []
        for n in range(count):
            node = first + n
            value = jnp.concatenate([loc[j, node] for j in range(bonds)], axis=0)
            store_up(2 * node, value)
            by_left = act_major(2 * node, current[2 * n])
            by_right = act_minor(2 * node, current[2 * n + 1])
            late.append((node, by_right))
            grown.append(close(by_left, by_right))
        envs.append(grown)
        first += count

    env = envs[-1][0]

    def env_copy(slot, n, hop):
        copy = pltpu.make_async_remote_copy(
            src_ref=esend.at[slot],
            dst_ref=erecv.at[n],
            send_sem=env_send.at[n],
            recv_sem=env_recv.at[n],
            device_id=(position ^ hop, mine),
            device_id_type=MESH,
        )
        copy.start()
        sends.append(copy)
        return copy

    def assemble(base, count, start, width):
        rows = []
        for j in range(bonds):
            rows.append(
                jnp.concatenate(
                    [raw[j, base + s, :, start : start + width] for s in range(count)], axis=1
                )
            )
        return jnp.concatenate(rows, axis=0)

    def top_value(k, r=0):
        base = ((position ^ r) >> (k + 1)) << (k + 1)
        return assemble(base, 2 << k, starts[k], cols >> (k + 1))

    def is_upper(k):
        return lax.rem(position >> k, 2) == 1

    def own_nodes(ks, more=()):
        values = [top_value(k) for k in ks]
        moved = permute([stacked(value) for value in values] + list(more))
        for n, k in enumerate(ks):
            chosen = jnp.where(is_upper(k), values[n], moved[n])
            store_up(2 * nodes + k, chosen)
            store_down(2 * nodes + k, chosen)
        return moved[len(ks) :]

    def local_values():
        return [
            jnp.concatenate([loc[j, node] for j in range(bonds)], axis=0) for node in range(nodes)
        ]

    esend[0] = env[0]
    group_envs = [env_copy(0, hop - 1, hop) for hop in reversed(range(1, span))]
    top_moves[0].forward()
    if joint < levels:
        far_moves[0].wait_recv()
        if joint + 1 < levels:
            far_copy(joint + 1)
        top_spread(joint)
    top_moves[0].finish()

    extra = 2 * nodes + levels
    others = {}
    locals_ = local_values()
    more = [stacked(value) for value in locals_] + [stacked(right) for _, right in late]
    more = own_nodes(range(joint), more)
    for k in range(joint):
        for r in range(2 << k, span, 2 << k):
            store_up(extra, top_value(k, r))
            others[k, r] = extra
            extra += 1
    for node in range(nodes):
        store_down(2 * node, locals_[node])
        store_down(2 * node + 1, more[node])
        keep(2 * node + 1, lanes_to_rows(more[nodes + node]))
    first_minor = act_minor(2 * nodes, env)
    for copy in group_envs:
        copy.wait_recv()
    pool = {0: env}
    for hop in range(1, span):
        pool[hop] = scaled(erecv[hop - 1])
    for k in range(joint):
        following = {}
        up = is_upper(k)
        for r in range(2 << k, span, 2 << k):
            item = others[k, r]
            near, far = pool[r], pool[r ^ (1 << k)]
            left = [jnp.where(up, x, y) for x, y in zip(far, near, strict=True)]
            right = [jnp.where(up, x, y) for x, y in zip(near, far, strict=True)]
            following[r] = close(act_major(item, left, False), act_minor(item, right))
        item = 2 * nodes + k
        minor = act_minor(item, pool[0]) if k else first_minor
        following[0] = close(act_major(item, pool[1 << k]), minor)
        pool = following
    env = pool[0]

    for k in range(joint, levels):
        esend[1 + k - joint] = env[0]
        copy = env_copy(1 + k - joint, span - 1 + k - joint, 1 << k)
        index = k - joint + 1
        top_moves[index].forward()
        if k + 1 < levels:
            far_moves[index].wait_recv()
            if k + 2 < levels:
                far_copy(k + 2)
            top_spread(k + 1)
        top_moves[index].finish()
        own_nodes([k])
        item = 2 * nodes + k
        minor = act_minor(item, env)
        if k == levels - 1:
            root = assemble(0, devices, starts[levels], cols >> levels)
            state = close(root, root)
        copy.wait_recv()
        env = close(act_major(item, scaled(erecv[span - 1 + k - joint])), minor)
    if joint == levels:
        root = assemble(0, devices, starts[levels], cols >> levels)
        state = close(root, root)

    top = env
    for k in range(levels - 1, -1, -1):
        marked = lax.rem(position + 1, 2 << k) == 1 << k
        top = [jnp.where(marked, x, y) for x, y in zip(state, top, strict=True)]
        state = descend(2 * nodes + k, state)
    flatten(normal(top), leaves + nodes)
    states = [state]
    for height in range(height_dev, 0, -1):
        count = leaves >> height
        offset = leaves - 2 * count
        below = []
        for n in range(count):
            node = offset + n
            flatten(normal(states[n]), leaves + node)
            below.append(descend(2 * node + 1, states[n]))
            below.append(descend(2 * node, states[n]))
        states = below
    for n in range(leaves):
        flatten(normal(states[n]), n)
    for copy in sends:
        copy.wait_send()


def place(leaves, nodes, packed, leaf_out, inner_out, top_out):
    first = 0
    for ref, count in ((leaf_out, leaves), (inner_out, nodes), (top_out, 1)):
        for n in range(count):
            for g in range(packed.shape[1]):
                spot = (n, slice(0, 1)) if ref is inner_out else (0, slice(n, n + 1))
                ref[spot + (slice(g * LANES, (g + 1) * LANES),)] = packed[first + n, g : g + 1, :]
        first += count


def body(cfg, leaf_metric, local_iso, top_iso):
    chi, leaves, devices, bonds = cfg
    cols = chi * chi
    nodes = leaves - 1
    levels = devices.bit_length() - 1
    joint = min(JOINT, levels)
    span = 1 << joint
    share = chi // bonds
    items = 2 * nodes + levels + span - 1 - joint
    moves = levels - joint + 1
    f32 = jnp.float32
    dma = pltpu.SemaphoreType.DMA
    vmem = pl.BlockSpec(memory_space=pltpu.VMEM)
    hbm = pl.BlockSpec(memory_space=pl.ANY)
    packed = pl.pallas_call(
        functools.partial(kernel, cfg),
        out_shape=jax.ShapeDtypeStruct((leaves + nodes + 1, cols // LANES, LANES), f32),
        in_specs=[hbm] * 3,
        out_specs=vmem,
        scratch_shapes=[
            pltpu.VMEM((1, leaves, cols), f32),
            pltpu.VMEM((bonds, devices, share, cols), f32),
            pltpu.VMEM((bonds, nodes, share, cols), f32),
            pltpu.VMEM((items, cols * chi // LANES, 2 * LANES), jnp.bfloat16),
            pltpu.VMEM((items, LANES, cols), jnp.bfloat16),
            pltpu.VMEM((items, cols * chi // LANES, 2 * LANES), jnp.bfloat16),
            pltpu.VMEM((items, 2 * LANES, cols * chi // LANES), jnp.bfloat16),
            pltpu.VMEM((chi, cols * chi // LANES), f32),
            pltpu.VMEM((cols, cols), jnp.bfloat16),
            pltpu.VMEM((moves, chi, LANES), f32),
            pltpu.VMEM((span - 2 + moves, chi, LANES), f32),
            dma((3,)),
            dma((nodes, bonds - 1)),
            dma((nodes, bonds - 1)),
            dma((span - 2 + moves,)),
            dma((span - 2 + moves,)),
            dma((moves, bonds - 1)),
            dma((moves, bonds - 1)),
            dma((span - 2 + moves,)),
            dma((span - 2 + moves,)),
        ],
        compiler_params=pltpu.CompilerParams(collective_id=0, has_side_effects=True),
        name="tree_sweep",
    )(leaf_metric, local_iso, top_iso)
    shapes = ((1, leaves, cols), (nodes, 1, cols), (1, 1, cols))
    leaf_rho, inner_rho, top_rho = pl.pallas_call(
        functools.partial(place, leaves, nodes),
        out_shape=tuple(jax.ShapeDtypeStruct(shape, f32) for shape in shapes),
        in_specs=[vmem],
        out_specs=(vmem,) * 3,
        name="place",
    )(packed)
    return leaf_rho, inner_rho.transpose(1, 0, 2), top_rho


def solution(mesh):
    devices, bonds = mesh.shape["leaf"], mesh.shape["bond"]
    spec = P("bond", "leaf", None)
    iso = P("leaf", "bond", None)

    def whole(leaf_metric, local_iso, top_iso):
        cfg = (local_iso.shape[1], leaf_metric.shape[1] // devices, devices, bonds)
        return jax.shard_map(
            functools.partial(body, cfg),
            mesh=mesh,
            in_specs=(spec, iso, iso),
            out_specs=(spec, spec, spec),
            check_vma=False,
        )(leaf_metric, local_iso, top_iso)

    return whole
```

```python
import functools

import jax
import jax.numpy as jnp
from jax import lax
from jax.experimental import pallas as pl
from jax.experimental.pallas import tpu as pltpu
from jax.sharding import PartitionSpec as P

LANES = 128
SUBLANES = 8
MESH = pl.DeviceIdType.MESH
EXACT = lax.Precision.HIGHEST
JOINT = 2


def mm(a, b):
    return jnp.dot(a, b, precision=EXACT, preferred_element_type=jnp.float32)


def dot(a, b):
    return jnp.dot(a, b, preferred_element_type=jnp.float32)


def dot_nt(a, b):
    return lax.dot_general(a, b, (((1,), (1,)), ((), ())), preferred_element_type=jnp.float32)


def halves(value):
    high = value.astype(jnp.bfloat16)
    low = (value - high.astype(jnp.float32)).astype(jnp.bfloat16)
    return high, low


def join_lanes(value):
    return value[:, :LANES] + value[:, LANES:]


def join_rows(value):
    half = value.shape[0] // 2
    return value[:half] + value[half:]


def kernel(
    cfg,
    leaf_hbm,
    local_hbm,
    top_hbm,
    out,
    leaf_ref,
    raw,
    loc,
    wk,
    wm,
    wq,
    yt,
    fbuf,
    perm,
    esend,
    erecv,
    own_sem,
    loc_send,
    loc_recv,
    leaf_send,
    leaf_recv,
    fwd_send,
    fwd_recv,
    env_send,
    env_recv,
):
    chi, leaves, devices, bonds = cfg
    cols = chi * chi
    rep = LANES // chi
    chunks = cols // LANES
    levels = devices.bit_length() - 1
    height_dev = leaves.bit_length() - 1
    nodes = leaves - 1
    joint = min(JOINT, levels)
    span = 1 << joint
    position = lax.axis_index("leaf")
    mine = lax.axis_index("bond")

    hops = list(range(1, span)) + [1 << k for k in range(joint, levels)]
    bits = [1 << b for b in reversed(range(bonds.bit_length() - 1))]

    barrier = pltpu.get_barrier_semaphore()
    for hop in hops:
        pl.semaphore_signal(barrier, inc=1, device_id=(position ^ hop, mine), device_id_type=MESH)
    for bit in bits:
        pl.semaphore_signal(barrier, inc=1, device_id=(position, mine ^ bit), device_id_type=MESH)
    own = [
        pltpu.make_async_copy(local_hbm, loc.at[mine], own_sem.at[0]),
        pltpu.make_async_copy(top_hbm.at[0], raw.at[mine, position], own_sem.at[1]),
        pltpu.make_async_copy(leaf_hbm, leaf_ref, own_sem.at[2]),
    ]
    for copy in own:
        copy.start()
    own[0].wait()
    own[1].wait()
    pl.semaphore_wait(barrier, len(hops) + len(bits))

    starts = [cols - (cols >> k) for k in range(levels + 1)]
    aligned = [s // LANES * LANES for s in starts]
    stops = [-(-s // LANES) * LANES for s in starts[1:-1]] + [cols]
    sends = []

    class Spread:
        def __init__(self, slices, send_sem, recv_sem):
            self.copies = {}
            self.left = set(range(1, bonds))
            for d in range(1, bonds):
                bit = d & -d
                ref = slices(mine ^ (d ^ bit))
                self.copies[d] = pltpu.make_async_remote_copy(
                    src_ref=ref,
                    dst_ref=ref,
                    send_sem=send_sem.at[d - 1],
                    recv_sem=recv_sem.at[d - 1],
                    device_id=(position, mine ^ bit),
                    device_id_type=MESH,
                )

        def start(self):
            for bit in bits:
                self.copies[bit].start()
                sends.append(self.copies[bit])
            return self

        def recv(self, d):
            if d in self.left:
                self.left.remove(d)
                self.copies[d].wait_recv()

        def forward(self):
            for bit in bits:
                for d in range(1, bonds):
                    if d & -d == bit and d != bit:
                        self.recv(d ^ bit)
                        self.copies[d].start()
                        sends.append(self.copies[d])

        def finish(self):
            for d in sorted(self.left):
                self.recv(d)

    def leaf_copy(n, hop, slots):
        copy = pltpu.make_async_remote_copy(
            src_ref=slots,
            dst_ref=slots,
            send_sem=leaf_send.at[n],
            recv_sem=leaf_recv.at[n],
            device_id=(position ^ hop, mine),
            device_id_type=MESH,
        )
        copy.start()
        sends.append(copy)
        return copy

    def block(level):
        return (position >> level) << level

    local_moves = []
    for n in range(nodes):
        local_moves.append(
            Spread(lambda j, n=n: loc.at[j, n], loc_send.at[n], loc_recv.at[n]).start()
        )
    group_moves = [
        leaf_copy(hop - 1, hop, raw.at[mine, position]) for hop in reversed(range(1, span))
    ]
    far_moves = []
    top_moves = []

    def far_copy(k):
        slots = raw.at[mine, pl.ds(block(k), 1 << k), :, aligned[k] : cols]
        far_moves.append(leaf_copy(span - 1 + k - joint, 1 << k, slots))

    def top_spread(k):
        if k < joint:
            base, count, lo, hi = block(joint), span, 0, stops[joint - 1]
        else:
            base, count, lo, hi = block(k + 1), 2 << k, aligned[k], stops[k]
        n = len(top_moves)
        top_moves.append(
            Spread(
                lambda j: raw.at[j, pl.ds(base, count), :, lo:hi], fwd_send.at[n], fwd_recv.at[n]
            ).start()
        )

    own[2].wait()

    row = lax.broadcasted_iota(jnp.int32, (chi, LANES), 0)
    lane = lax.broadcasted_iota(jnp.int32, (chi, LANES), 1)
    group = lane // chi
    row_mask = group == lax.rem(row, rep)
    diag_mask = row == lane
    big_row = lax.broadcasted_iota(jnp.int32, (LANES, LANES), 0)
    big_lane = lax.broadcasted_iota(jnp.int32, (LANES, LANES), 1)
    block_mask = big_row // chi == big_lane // chi
    spread = (
        lax.broadcasted_iota(jnp.int32, (chi, chunks), 0) // rep
        == lax.broadcasted_iota(jnp.int32, (chi, chunks), 1)
    ).astype(jnp.float32)
    sub = chi // rep
    spread_lanes = [
        (lane + start) // sub for start in range(0, chi * sub, LANES)
    ]
    unit_mask = lax.rem(
        lax.broadcasted_iota(jnp.int32, (sub, chi * sub), 1), sub
    ) == lax.broadcasted_iota(jnp.int32, (sub, chi * sub), 0)
    column = lax.broadcasted_iota(jnp.int32, (chi, cols), 1)
    swapped_column = lax.broadcasted_iota(jnp.int32, (chi, cols), 0) * chi

    @pl.loop(0, chi)
    def _(a):
        perm[pl.ds(pl.multiple_of(a * chi, chi), chi), :] = (
            (column == swapped_column + a).astype(jnp.float32).astype(jnp.bfloat16)
        )

    part_group = lax.broadcasted_iota(jnp.int32, (chunks * sub, LANES), 1) // chi

    def swap_groups(value):
        parts = [
            jnp.concatenate(
                [value[g * chi + v * sub : g * chi + (v + 1) * sub] for g in range(chunks)], axis=0
            )
            for v in range(rep)
        ]
        bit = 1
        while bit < rep:
            lower = lax.rem(part_group // bit, 2) == 0
            for a in range(rep):
                if a & bit == 0:
                    one, two = parts[a], parts[a | bit]
                    parts[a] = jnp.where(lower, one, pltpu.roll(two, bit * chi, 1))
                    parts[a | bit] = jnp.where(lower, pltpu.roll(one, LANES - bit * chi, 1), two)
            bit *= 2
        return jnp.concatenate(
            [parts[v][g * sub : (g + 1) * sub] for g in range(chunks) for v in range(rep)], axis=0
        )

    def fold(value):
        shift = chi
        while shift < LANES:
            value = value + pltpu.roll(value, shift, 1)
            shift *= 2
        return value

    def scaled(matrix):
        trace = jnp.sum(jnp.where(diag_mask, matrix, 0.0), axis=(0, 1), keepdims=True)
        return matrix, chi / trace

    def normal(pair):
        return pair[0] * pair[1]

    def unflatten(line):
        tile = jnp.concatenate(
            [line[:, g * LANES : (g + 1) * LANES] for g in range(chunks)], axis=0
        )
        return fold(jnp.where(row_mask, mm(spread, tile), 0.0))

    def lanes_to_rows(value):
        return jnp.concatenate(
            [value[:, g * LANES : (g + 1) * LANES] for g in range(chunks)], axis=0
        )

    def rows_to_lanes(value):
        return jnp.concatenate([value[g * chi : (g + 1) * chi] for g in range(chunks)], axis=1)

    def stacked(value):
        return jnp.concatenate(halves(value), axis=0)

    def permute(parts):
        stack = parts[0] if len(parts) == 1 else jnp.concatenate(parts, axis=0)
        moved = dot(stack, perm[...])
        return [join_rows(moved[n * 2 * chi : (n + 1) * 2 * chi]) for n in range(len(parts))]

    def store_down(item, value):
        high, low = halves(value)
        wm[item] = jnp.concatenate([high, low] * (rep // 2), axis=0)

    def store_up(item, value):
        high, low = halves(value)
        wk[item] = jnp.concatenate([lanes_to_rows(high), lanes_to_rows(low)], axis=1)
        wq[item] = jnp.concatenate(halves(swap_groups(lanes_to_rows(value))), axis=1)

    def keep(item, acted):
        yt[item] = stacked(acted.T)

    def for_minor(env):
        block = jnp.where(block_mask, jnp.concatenate([env[0]] * rep, axis=0), 0.0)
        pair = jnp.concatenate(halves(block), axis=1)
        return jnp.concatenate([pair, pair], axis=0), env[1]

    def act_minor(item, env):
        return rows_to_lanes(join_lanes(dot(wk[item], env[0])) * env[1])

    def for_major(env):
        fbuf[...] = jnp.concatenate(
            [jnp.take_along_axis(env[0], index, axis=1) for index in spread_lanes], axis=1
        )
        wide = jnp.concatenate(
            [
                jnp.where(unit_mask, jnp.broadcast_to(fbuf[y : y + 1, :], unit_mask.shape), 0.0)
                for y in range(chi)
            ],
            axis=0,
        )
        return jnp.concatenate(halves(wide), axis=0), env[1]

    def act_major(item, env, down=True):
        acted = dot(env[0], wq[item])
        acted = swap_groups(join_lanes(join_rows(acted)) * env[1])
        if down:
            keep(item, acted)
        return rows_to_lanes(acted)

    def close(left, right):
        high, low = halves(right)
        wide = jnp.concatenate([high] * rep + [low] * rep, axis=0)
        tall = jnp.concatenate(halves(left), axis=0)
        return scaled(join_lanes(join_rows(dot_nt(tall, wide))))

    def mix(item, state):
        state, scale = state
        high = state.astype(jnp.bfloat16).astype(jnp.float32)
        parts = jnp.where(group < rep // 2, high, state - high).astype(jnp.bfloat16)
        mixed = lanes_to_rows(dot(parts, wm[item]) * scale)
        return jnp.concatenate(halves(mixed), axis=1)

    def descend(item, state, mixed=None):
        if mixed is None:
            mixed = mix(item, state)
        square = dot(yt[item], mixed)
        square = jnp.where(block_mask, join_lanes(join_rows(square)), 0.0)
        total = square[:chi]
        for i in range(1, rep):
            total = total + square[i * chi : (i + 1) * chi]
        return scaled(fold(total))

    envs = [[(unflatten(leaf_ref[0, n : n + 1, :]), 1.0) for n in range(leaves)]]
    for move in local_moves:
        move.forward()
    for move in group_moves:
        move.wait_recv()
    if joint < levels:
        far_copy(joint)
    top_spread(0)

    late = []
    first = 0
    for height in range(1, height_dev + 1):
        current = envs[-1]
        count = leaves >> height
        majors = [for_major(current[2 * n]) for n in range(count)]
        minors = [for_minor(current[2 * n + 1]) for n in range(count)]
        for n in range(count):
            local_moves[first + n].finish()
        grown = []
        for n in range(count):
            node = first + n
            value = jnp.concatenate([loc[j, node] for j in range(bonds)], axis=0)
            store_up(2 * node, value)
            by_left = act_major(2 * node, majors[n])
            by_right = act_minor(2 * node, minors[n])
            late.append((node, by_right))
            grown.append(close(by_left, by_right))
        envs.append(grown)
        first += count

    env = envs[-1][0]

    def env_copy(slot, n, hop):
        copy = pltpu.make_async_remote_copy(
            src_ref=esend.at[slot],
            dst_ref=erecv.at[n],
            send_sem=env_send.at[n],
            recv_sem=env_recv.at[n],
            device_id=(position ^ hop, mine),
            device_id_type=MESH,
        )
        copy.start()
        sends.append(copy)
        return copy

    def assemble(base, count, start, width):
        rows = []
        for j in range(bonds):
            rows.append(
                jnp.concatenate(
                    [raw[j, base + s, :, start : start + width] for s in range(count)], axis=1
                )
            )
        return jnp.concatenate(rows, axis=0)

    def top_value(k, r=0):
        base = ((position ^ r) >> (k + 1)) << (k + 1)
        return assemble(base, 2 << k, starts[k], cols >> (k + 1))

    def is_upper(k):
        return lax.rem(position >> k, 2) == 1

    def own_nodes(ks, more=()):
        values = [top_value(k) for k in ks]
        moved = permute([stacked(value) for value in values] + list(more))
        for n, k in enumerate(ks):
            chosen = jnp.where(is_upper(k), values[n], moved[n])
            store_up(2 * nodes + k, chosen)
            store_down(2 * nodes + k, chosen)
        return moved[len(ks) :]

    def local_values():
        return [
            jnp.concatenate([loc[j, node] for j in range(bonds)], axis=0) for node in range(nodes)
        ]

    esend[0] = env[0]
    group_envs = [env_copy(0, hop - 1, hop) for hop in reversed(range(1, span))]
    top_moves[0].forward()
    if joint < levels:
        far_moves[0].wait_recv()
        if joint + 1 < levels:
            far_copy(joint + 1)
        top_spread(joint)
    top_moves[0].finish()

    extra = 2 * nodes + levels
    others = {}
    locals_ = local_values()
    more = [stacked(value) for value in locals_] + [stacked(right) for _, right in late]
    more = own_nodes(range(joint), more)
    for k in range(joint):
        for r in range(2 << k, span, 2 << k):
            store_up(extra, top_value(k, r))
            others[k, r] = extra
            extra += 1
    for node in range(nodes):
        store_down(2 * node, locals_[node])
        store_down(2 * node + 1, more[node])
        keep(2 * node + 1, lanes_to_rows(more[nodes + node]))
    first_minor = act_minor(2 * nodes, for_minor(env))
    for copy in group_envs:
        copy.wait_recv()
    pool = {0: env}
    for hop in range(1, span):
        pool[hop] = scaled(erecv[hop - 1])
    for k in range(joint):
        following = {}
        up = is_upper(k)
        for r in range(2 << k, span, 2 << k):
            item = others[k, r]
            near, far = pool[r], pool[r ^ (1 << k)]
            left = [jnp.where(up, x, y) for x, y in zip(far, near, strict=True)]
            right = [jnp.where(up, x, y) for x, y in zip(near, far, strict=True)]
            following[r] = close(
                act_major(item, for_major(left), False), act_minor(item, for_minor(right))
            )
        item = 2 * nodes + k
        minor = act_minor(item, for_minor(pool[0])) if k else first_minor
        following[0] = close(act_major(item, for_major(pool[1 << k])), minor)
        pool = following
    env = pool[0]

    for k in range(joint, levels):
        esend[1 + k - joint] = env[0]
        copy = env_copy(1 + k - joint, span - 1 + k - joint, 1 << k)
        index = k - joint + 1
        top_moves[index].forward()
        if k + 1 < levels:
            far_moves[index].wait_recv()
            if k + 2 < levels:
                far_copy(k + 2)
            top_spread(k + 1)
        top_moves[index].finish()
        own_nodes([k])
        item = 2 * nodes + k
        minor = act_minor(item, for_minor(env))
        if k == levels - 1:
            root = assemble(0, devices, starts[levels], cols >> levels)
            state = close(root, root)
            mixed = mix(item, state)
        copy.wait_recv()
        env = close(act_major(item, for_major(scaled(erecv[span - 1 + k - joint]))), minor)
    if joint == levels:
        root = assemble(0, devices, starts[levels], cols >> levels)
        state = close(root, root)
        mixed = mix(2 * nodes + levels - 1, state)

    top = env
    for k in range(levels - 1, -1, -1):
        marked = lax.rem(position + 1, 2 << k) == 1 << k
        top = [jnp.where(marked, x, y) for x, y in zip(state, top, strict=True)]
        state = descend(2 * nodes + k, state, mixed if k == levels - 1 else None)
    out[leaves + nodes] = normal(top)
    states = [state]
    for height in range(height_dev, 0, -1):
        count = leaves >> height
        offset = leaves - 2 * count
        below = []
        for n in range(count):
            node = offset + n
            out[leaves + node] = normal(states[n])
            below.append(descend(2 * node + 1, states[n]))
            below.append(descend(2 * node, states[n]))
        states = below
    for n in range(leaves):
        out[n] = normal(states[n])
    for copy in sends:
        copy.wait_send()


def place(leaves, nodes, packed, leaf_out, inner_out, top_out):
    chi = packed.shape[1]
    rep = LANES // chi
    row = lax.broadcasted_iota(jnp.int32, (SUBLANES, LANES), 0)
    row_mask = lax.broadcasted_iota(jnp.int32, (SUBLANES, LANES), 1) // chi == lax.rem(row, rep)
    first = 0
    for ref, count in ((leaf_out, leaves), (inner_out, nodes), (top_out, 1)):
        for n in range(count):
            for v in range(0, chi, SUBLANES):
                value = jnp.where(row_mask, packed[first + n, v : v + SUBLANES], 0.0)
                step = 1
                while step < rep:
                    value = value + pltpu.roll(value, SUBLANES - step, 0)
                    step *= 2
                for r in range(0, SUBLANES, rep):
                    g = (v + r) // rep
                    spot = (n, slice(0, 1)) if ref is inner_out else (0, slice(n, n + 1))
                    ref[spot + (slice(g * LANES, (g + 1) * LANES),)] = value[r : r + 1]
        first += count


def body(cfg, leaf_metric, local_iso, top_iso):
    chi, leaves, devices, bonds = cfg
    cols = chi * chi
    nodes = leaves - 1
    levels = devices.bit_length() - 1
    joint = min(JOINT, levels)
    span = 1 << joint
    share = chi // bonds
    items = 2 * nodes + levels + span - 1 - joint
    moves = levels - joint + 1
    f32 = jnp.float32
    dma = pltpu.SemaphoreType.DMA
    vmem = pl.BlockSpec(memory_space=pltpu.VMEM)
    hbm = pl.BlockSpec(memory_space=pl.ANY)
    packed = pl.pallas_call(
        functools.partial(kernel, cfg),
        out_shape=pltpu.VMEM((leaves + nodes + 1, chi, LANES), f32),
        in_specs=[hbm] * 3,
        out_specs=vmem,
        scratch_shapes=[
            pltpu.VMEM((1, leaves, cols), f32),
            pltpu.VMEM((bonds, devices, share, cols), f32),
            pltpu.VMEM((bonds, nodes, share, cols), f32),
            pltpu.VMEM((items, cols * chi // LANES, 2 * LANES), jnp.bfloat16),
            pltpu.VMEM((items, LANES, cols), jnp.bfloat16),
            pltpu.VMEM((items, cols * chi // LANES, 2 * LANES), jnp.bfloat16),
            pltpu.VMEM((items, 2 * LANES, cols * chi // LANES), jnp.bfloat16),
            pltpu.VMEM((chi, cols * chi // LANES), f32),
            pltpu.VMEM((cols, cols), jnp.bfloat16),
            pltpu.VMEM((moves, chi, LANES), f32),
            pltpu.VMEM((span - 2 + moves, chi, LANES), f32),
            dma((3,)),
            dma((nodes, bonds - 1)),
            dma((nodes, bonds - 1)),
            dma((span - 2 + moves,)),
            dma((span - 2 + moves,)),
            dma((moves, bonds - 1)),
            dma((moves, bonds - 1)),
            dma((span - 2 + moves,)),
            dma((span - 2 + moves,)),
        ],
        compiler_params=pltpu.CompilerParams(collective_id=0, has_side_effects=True),
        name="tree_sweep",
    )(leaf_metric, local_iso, top_iso)
    shapes = ((1, leaves, cols), (nodes, 1, cols), (1, 1, cols))
    leaf_rho, inner_rho, top_rho = pl.pallas_call(
        functools.partial(place, leaves, nodes),
        out_shape=tuple(jax.ShapeDtypeStruct(shape, f32) for shape in shapes),
        in_specs=[vmem],
        out_specs=(vmem,) * 3,
        name="place",
    )(pltpu.with_memory_space_constraint(packed, pltpu.VMEM))
    return leaf_rho, inner_rho.transpose(1, 0, 2), top_rho


def solution(mesh):
    devices, bonds = mesh.shape["leaf"], mesh.shape["bond"]
    spec = P("bond", "leaf", None)
    iso = P("leaf", "bond", None)

    def whole(leaf_metric, local_iso, top_iso):
        cfg = (local_iso.shape[1], leaf_metric.shape[1] // devices, devices, bonds)
        return jax.shard_map(
            functools.partial(body, cfg),
            mesh=mesh,
            in_specs=(spec, iso, iso),
            out_specs=(spec, spec, spec),
            check_vma=False,
        )(leaf_metric, local_iso, top_iso)

    return whole
```

```python
import functools

import jax
import jax.numpy as jnp
from jax import lax
from jax.experimental import pallas as pl
from jax.experimental.pallas import tpu as pltpu
from jax.sharding import PartitionSpec as P

LANES = 128
SUBLANES = 8
MESH = pl.DeviceIdType.MESH
EXACT = lax.Precision.HIGHEST
JOINT = 2


def mm(a, b):
    return jnp.dot(a, b, precision=EXACT, preferred_element_type=jnp.float32)


def dot(a, b):
    return jnp.dot(a, b, preferred_element_type=jnp.float32)


def dot_nt(a, b):
    return lax.dot_general(a, b, (((1,), (1,)), ((), ())), preferred_element_type=jnp.float32)


def halves(value):
    high = value.astype(jnp.bfloat16)
    low = (value - high.astype(jnp.float32)).astype(jnp.bfloat16)
    return high, low


def join_lanes(value):
    return value[:, :LANES] + value[:, LANES:]


def join_rows(value):
    half = value.shape[0] // 2
    return value[:half] + value[half:]


def kernel(
    cfg,
    leaf_hbm,
    local_hbm,
    top_hbm,
    out,
    leaf_ref,
    raw,
    loc,
    wk,
    wm,
    wq,
    yt,
    fbuf,
    perm,
    esend,
    erecv,
    own_sem,
    loc_send,
    loc_recv,
    leaf_send,
    leaf_recv,
    fwd_send,
    fwd_recv,
    env_send,
    env_recv,
):
    chi, leaves, devices, bonds = cfg
    cols = chi * chi
    rep = LANES // chi
    chunks = cols // LANES
    levels = devices.bit_length() - 1
    height_dev = leaves.bit_length() - 1
    nodes = leaves - 1
    joint = min(JOINT, levels)
    span = 1 << joint
    position = lax.axis_index("leaf")
    mine = lax.axis_index("bond")

    hops = list(range(1, span)) + [1 << k for k in range(joint, levels)]
    bits = [1 << b for b in reversed(range(bonds.bit_length() - 1))]

    barrier = pltpu.get_barrier_semaphore()
    for hop in hops:
        pl.semaphore_signal(barrier, inc=1, device_id=(position ^ hop, mine), device_id_type=MESH)
    for bit in bits:
        pl.semaphore_signal(barrier, inc=1, device_id=(position, mine ^ bit), device_id_type=MESH)
    own = [
        pltpu.make_async_copy(local_hbm, loc.at[mine], own_sem.at[0]),
        pltpu.make_async_copy(top_hbm.at[0], raw.at[mine, position], own_sem.at[1]),
        pltpu.make_async_copy(leaf_hbm, leaf_ref, own_sem.at[2]),
    ]
    for copy in own:
        copy.start()
    own[0].wait()
    own[1].wait()
    pl.semaphore_wait(barrier, len(hops) + len(bits))

    starts = [cols - (cols >> k) for k in range(levels + 1)]
    aligned = [s // LANES * LANES for s in starts]
    stops = [-(-s // LANES) * LANES for s in starts[1:-1]] + [cols]
    sends = []
    spreads = []

    class Spread:
        def __init__(self, slices, send_sem, recv_sem):
            self.copies = {}
            self.left = set(range(1, bonds))
            for d in range(1, bonds):
                bit = d & -d
                ref = slices(mine ^ (d ^ bit))
                self.copies[d] = pltpu.make_async_remote_copy(
                    src_ref=ref,
                    dst_ref=ref,
                    send_sem=send_sem.at[d - 1],
                    recv_sem=recv_sem.at[d - 1],
                    device_id=(position, mine ^ bit),
                    device_id_type=MESH,
                )

        def start(self):
            for bit in bits:
                self.copies[bit].start()
                sends.append(self.copies[bit])
            return self

        def recv(self, d):
            if d in self.left:
                self.left.remove(d)
                self.copies[d].wait_recv()

        def forward(self):
            for bit in bits:
                for d in range(1, bonds):
                    if d & -d == bit and d != bit:
                        self.recv(d ^ bit)
                        self.copies[d].start()
                        sends.append(self.copies[d])

        def finish(self):
            for d in sorted(self.left):
                self.recv(d)

    def leaf_copy(n, hop, slots):
        copy = pltpu.make_async_remote_copy(
            src_ref=slots,
            dst_ref=slots,
            send_sem=leaf_send.at[n],
            recv_sem=leaf_recv.at[n],
            device_id=(position ^ hop, mine),
            device_id_type=MESH,
        )
        copy.start()
        sends.append(copy)
        return copy

    def block(level):
        return (position >> level) << level

    local_moves = []
    for n in range(nodes):
        local_moves.append(
            Spread(lambda j, n=n: loc.at[j, n], loc_send.at[n], loc_recv.at[n]).start()
        )
    group_moves = [
        leaf_copy(hop - 1, hop, raw.at[mine, position]) for hop in reversed(range(1, span))
    ]
    far_moves = []
    top_moves = []

    def far_copy(k):
        slots = raw.at[mine, pl.ds(block(k), 1 << k), :, aligned[k] : cols]
        far_moves.append(leaf_copy(span - 1 + k - joint, 1 << k, slots))

    def top_spread(k):
        if k < joint:
            base, count, lo, hi = block(joint), span, 0, stops[joint - 1]
        else:
            base, count, lo, hi = block(k + 1), 2 << k, aligned[k], stops[k]
        n = len(top_moves)
        top_moves.append(
            Spread(
                lambda j: raw.at[j, pl.ds(base, count), :, lo:hi], fwd_send.at[n], fwd_recv.at[n]
            ).start()
        )

    own[2].wait()

    row = lax.broadcasted_iota(jnp.int32, (chi, LANES), 0)
    lane = lax.broadcasted_iota(jnp.int32, (chi, LANES), 1)
    group = lane // chi
    row_mask = group == lax.rem(row, rep)
    diag_mask = row == lane
    big_row = lax.broadcasted_iota(jnp.int32, (LANES, LANES), 0)
    big_lane = lax.broadcasted_iota(jnp.int32, (LANES, LANES), 1)
    block_mask = big_row // chi == big_lane // chi
    spread = (
        lax.broadcasted_iota(jnp.int32, (chi, chunks), 0) // rep
        == lax.broadcasted_iota(jnp.int32, (chi, chunks), 1)
    ).astype(jnp.float32)
    sub = chi // rep
    part_lane = group[:sub]
    group_lanes = [lax.rem(lane[:sub], chi) + v * chi for v in range(rep)]
    spread_lanes = [
        (lane + start) // sub for start in range(0, chi * sub, LANES)
    ]
    unit_mask = lax.rem(
        lax.broadcasted_iota(jnp.int32, (sub, chi * sub), 1), sub
    ) == lax.broadcasted_iota(jnp.int32, (sub, chi * sub), 0)
    column = lax.broadcasted_iota(jnp.int32, (chi, cols), 1)
    swapped_column = lax.broadcasted_iota(jnp.int32, (chi, cols), 0) * chi

    @pl.loop(0, chi)
    def _(a):
        perm[pl.ds(pl.multiple_of(a * chi, chi), chi), :] = (
            (column == swapped_column + a).astype(jnp.float32).astype(jnp.bfloat16)
        )

    part_group = lax.broadcasted_iota(jnp.int32, (chunks * sub, LANES), 1) // chi

    def swap_groups(value):
        parts = [
            jnp.concatenate(
                [value[g * chi + v * sub : g * chi + (v + 1) * sub] for g in range(chunks)], axis=0
            )
            for v in range(rep)
        ]
        bit = 1
        while bit < rep:
            lower = lax.rem(part_group // bit, 2) == 0
            for a in range(rep):
                if a & bit == 0:
                    one, two = parts[a], parts[a | bit]
                    parts[a] = jnp.where(lower, one, pltpu.roll(two, bit * chi, 1))
                    parts[a | bit] = jnp.where(lower, pltpu.roll(one, LANES - bit * chi, 1), two)
            bit *= 2
        return jnp.concatenate(
            [parts[v][g * sub : (g + 1) * sub] for g in range(chunks) for v in range(rep)], axis=0
        )

    def fold(value):
        shift = chi
        while shift < LANES:
            value = value + pltpu.roll(value, shift, 1)
            shift *= 2
        return value

    def scaled(matrix):
        trace = jnp.sum(jnp.where(diag_mask, matrix, 0.0), axis=(0, 1), keepdims=True)
        return matrix, chi / trace

    def normal(pair):
        return pair[0] * pair[1]

    def unflatten(line):
        tile = jnp.concatenate(
            [line[:, g * LANES : (g + 1) * LANES] for g in range(chunks)], axis=0
        )
        return fold(jnp.where(row_mask, mm(spread, tile), 0.0))

    def lanes_to_rows(value):
        return jnp.concatenate(
            [value[:, g * LANES : (g + 1) * LANES] for g in range(chunks)], axis=0
        )

    def rows_to_lanes(value):
        return jnp.concatenate([value[g * chi : (g + 1) * chi] for g in range(chunks)], axis=1)

    def packed(matrix):
        value = matrix[:sub]
        for v in range(1, rep):
            value = jnp.where(part_lane == v, matrix[v * sub : (v + 1) * sub], value)
        return value

    def unpacked(value):
        return jnp.concatenate(
            [jnp.take_along_axis(value, index, axis=1) for index in group_lanes], axis=0
        )

    def stacked(value):
        return jnp.concatenate(halves(value), axis=0)

    def permute(parts):
        stack = parts[0] if len(parts) == 1 else jnp.concatenate(parts, axis=0)
        moved = dot(stack, perm[...])
        return [join_rows(moved[n * 2 * chi : (n + 1) * 2 * chi]) for n in range(len(parts))]

    def store_down(item, value):
        high, low = halves(value)
        wm[item] = jnp.concatenate([high, low] * (rep // 2), axis=0)

    def store_up(item, value):
        high, low = halves(value)
        wk[item] = jnp.concatenate([lanes_to_rows(high), lanes_to_rows(low)], axis=1)
        wq[item] = jnp.concatenate(halves(swap_groups(lanes_to_rows(value))), axis=1)

    def keep(item, acted):
        yt[item] = stacked(acted.T)

    def for_minor(env):
        block = jnp.where(block_mask, jnp.concatenate([env[0]] * rep, axis=0), 0.0)
        pair = jnp.concatenate(halves(block), axis=1)
        return jnp.concatenate([pair, pair], axis=0), env[1]

    def act_minor(item, env):
        return rows_to_lanes(join_lanes(dot(wk[item], env[0])) * env[1])

    def for_major(env):
        slot = fbuf.at[len(spreads) % fbuf.shape[0]]
        spreads.append(slot)
        slot[...] = jnp.concatenate(
            [jnp.take_along_axis(env[0], index, axis=1) for index in spread_lanes], axis=1
        )
        wide = jnp.concatenate(
            [
                jnp.where(unit_mask, jnp.broadcast_to(slot[y : y + 1, :], unit_mask.shape), 0.0)
                for y in range(chi)
            ],
            axis=0,
        )
        return jnp.concatenate(halves(wide), axis=0), env[1]

    def act_major(item, env, down=True):
        acted = dot(env[0], wq[item])
        acted = swap_groups(join_lanes(join_rows(acted)) * env[1])
        if down:
            keep(item, acted)
        return rows_to_lanes(acted)

    def close(left, right):
        high, low = halves(right)
        wide = jnp.concatenate([high] * rep + [low] * rep, axis=0)
        tall = jnp.concatenate(halves(left), axis=0)
        return scaled(join_lanes(join_rows(dot_nt(tall, wide))))

    def mix(item, state):
        state, scale = state
        high = state.astype(jnp.bfloat16).astype(jnp.float32)
        parts = jnp.where(group < rep // 2, high, state - high).astype(jnp.bfloat16)
        mixed = lanes_to_rows(dot(parts, wm[item]) * scale)
        return jnp.concatenate(halves(mixed), axis=1)

    def settle(square):
        square = jnp.where(block_mask, join_lanes(join_rows(square)), 0.0)
        total = square[:chi]
        for i in range(1, rep):
            total = total + square[i * chi : (i + 1) * chi]
        return scaled(fold(total))

    def descend(items, mixes):
        squares = [dot(yt[item], mixed) for item, mixed in zip(items, mixes, strict=True)]
        return [settle(square) for square in squares]

    envs = [[(unflatten(leaf_ref[0, n : n + 1, :]), 1.0) for n in range(leaves)]]
    early = leaves >> 1
    for move in local_moves[:early]:
        move.forward()
    for move in group_moves:
        move.wait_recv()
    if joint < levels:
        far_copy(joint)
    top_spread(0)
    for move in local_moves[early:]:
        move.forward()

    late = []
    first = 0
    for height in range(1, height_dev + 1):
        current = envs[-1]
        count = leaves >> height
        majors = [for_major(current[2 * n]) for n in range(count)]
        minors = [for_minor(current[2 * n + 1]) for n in range(count)]
        for n in range(count):
            local_moves[first + n].finish()
        for n in range(count):
            node = first + n
            store_up(2 * node, jnp.concatenate([loc[j, node] for j in range(bonds)], axis=0))
        lefts = [act_major(2 * (first + n), majors[n], False) for n in range(count)]
        rights = [act_minor(2 * (first + n), minors[n]) for n in range(count)]
        late.extend(zip(lefts, rights, strict=True))
        grown = [close(lefts[n], rights[n]) for n in range(count)]
        envs.append(grown)
        first += count

    env = envs[-1][0]

    def env_copy(slot, n, hop):
        copy = pltpu.make_async_remote_copy(
            src_ref=esend.at[slot],
            dst_ref=erecv.at[n],
            send_sem=env_send.at[n],
            recv_sem=env_recv.at[n],
            device_id=(position ^ hop, mine),
            device_id_type=MESH,
        )
        copy.start()
        sends.append(copy)
        return copy

    def assemble(base, count, start, width):
        rows = []
        for j in range(bonds):
            rows.append(
                jnp.concatenate(
                    [raw[j, base + s, :, start : start + width] for s in range(count)], axis=1
                )
            )
        return jnp.concatenate(rows, axis=0)

    def top_value(k, r=0):
        base = ((position ^ r) >> (k + 1)) << (k + 1)
        return assemble(base, 2 << k, starts[k], cols >> (k + 1))

    def is_upper(k):
        return lax.rem(position >> k, 2) == 1

    def own_nodes(ks):
        values = [top_value(k) for k in ks]
        moved = permute([stacked(value) for value in values])
        for n, k in enumerate(ks):
            chosen = jnp.where(is_upper(k), values[n], moved[n])
            store_up(2 * nodes + k, chosen)
            store_down(2 * nodes + k, chosen)

    def local_values():
        return [
            jnp.concatenate([loc[j, node] for j in range(bonds)], axis=0) for node in range(nodes)
        ]

    esend[0] = packed(env[0])
    group_envs = [env_copy(0, hop - 1, hop) for hop in reversed(range(1, span))]

    top_moves[0].forward()
    locals_ = local_values()
    more = permute([stacked(value) for value in locals_] + [stacked(right) for _, right in late])
    for node in range(nodes):
        store_down(2 * node, locals_[node])
        store_down(2 * node + 1, more[node])
        keep(2 * node, lanes_to_rows(late[node][0]))
        keep(2 * node + 1, lanes_to_rows(more[nodes + node]))
    if joint < levels:
        far_moves[0].wait_recv()
        if joint + 1 < levels:
            far_copy(joint + 1)
        top_spread(joint)
    top_moves[0].finish()

    extra = 2 * nodes + levels
    others = {}
    tops = [top_value(k) for k in range(joint)]
    for k in range(joint):
        store_up(2 * nodes + k, tops[k])
        others[k, 0] = 2 * nodes + k
        for r in range(2 << k, span, 2 << k):
            store_up(extra, top_value(k, r))
            others[k, r] = extra
            extra += 1
    for copy in group_envs:
        copy.wait_recv()
    pool = {0: env}
    for hop in range(1, span):
        pool[hop] = scaled(unpacked(erecv[hop - 1]))
    acted = []
    for k in range(joint):
        up = is_upper(k)
        sides = {}
        for r in range(0, span, 2 << k):
            near, far = pool[r], pool[r ^ (1 << k)]
            left = [jnp.where(up, x, y) for x, y in zip(far, near, strict=True)]
            right = [jnp.where(up, x, y) for x, y in zip(near, far, strict=True)]
            sides[r] = for_major(left), for_minor(right)
        lefts = {r: act_major(others[k, r], side[0], False) for r, side in sides.items()}
        rights = {r: act_minor(others[k, r], side[1]) for r, side in sides.items()}
        following = {r: close(lefts[r], rights[r]) for r in sides}
        acted.append((lefts[0], rights[0]))
        pool = following
    env = pool[0]

    for k in range(joint, levels):
        esend[1 + k - joint] = packed(env[0])
        copy = env_copy(1 + k - joint, span - 1 + k - joint, 1 << k)
        index = k - joint + 1
        top_moves[index].forward()
        if k == joint:
            moved = permute(
                [stacked(value) for value in tops] + [stacked(right) for _, right in acted]
            )
            for n in range(joint):
                up = is_upper(n)
                store_down(2 * nodes + n, jnp.where(up, tops[n], moved[n]))
                chosen = jnp.where(up, acted[n][0], moved[joint + n])
                keep(2 * nodes + n, lanes_to_rows(chosen))
        if k + 1 < levels:
            far_moves[index].wait_recv()
            if k + 2 < levels:
                far_copy(k + 2)
            top_spread(k + 1)
        top_moves[index].finish()
        own_nodes([k])
        item = 2 * nodes + k
        minor = act_minor(item, for_minor(env))
        if k == levels - 1:
            root = assemble(0, devices, starts[levels], cols >> levels)
            state = close(root, root)
            mixed = mix(item, state)
        copy.wait_recv()
        env = close(act_major(item, for_major(scaled(unpacked(erecv[span - 1 + k - joint])))), minor)
    if joint == levels:
        root = assemble(0, devices, starts[levels], cols >> levels)
        state = close(root, root)
        mixed = mix(2 * nodes + levels - 1, state)

    top = env
    for k in range(levels - 1, -1, -1):
        marked = lax.rem(position + 1, 2 << k) == 1 << k
        top = [jnp.where(marked, x, y) for x, y in zip(state, top, strict=True)]
        (state,) = descend(
            [2 * nodes + k], [mixed if k == levels - 1 else mix(2 * nodes + k, state)]
        )
    out[leaves + nodes] = normal(top)
    states = [state]
    for height in range(height_dev, 0, -1):
        count = leaves >> height
        offset = leaves - 2 * count
        for n in range(count):
            out[leaves + offset + n] = normal(states[n])
        items = [2 * (offset + n) + 1 - side for n in range(count) for side in range(2)]
        states = descend(items, [mix(item, states[n // 2]) for n, item in enumerate(items)])
    for n in range(leaves):
        out[n] = normal(states[n])
    for copy in sends:
        copy.wait_send()


def place(leaves, nodes, packed, leaf_out, inner_out, top_out):
    chi = packed.shape[1]
    rep = LANES // chi
    row = lax.broadcasted_iota(jnp.int32, (SUBLANES, LANES), 0)
    row_mask = lax.broadcasted_iota(jnp.int32, (SUBLANES, LANES), 1) // chi == lax.rem(row, rep)
    first = 0
    for ref, count in ((leaf_out, leaves), (inner_out, nodes), (top_out, 1)):
        for n in range(count):
            for v in range(0, chi, SUBLANES):
                value = jnp.where(row_mask, packed[first + n, v : v + SUBLANES], 0.0)
                step = 1
                while step < rep:
                    value = value + pltpu.roll(value, SUBLANES - step, 0)
                    step *= 2
                for r in range(0, SUBLANES, rep):
                    g = (v + r) // rep
                    spot = (n, slice(0, 1)) if ref is inner_out else (0, slice(n, n + 1))
                    ref[spot + (slice(g * LANES, (g + 1) * LANES),)] = value[r : r + 1]
        first += count


def body(cfg, leaf_metric, local_iso, top_iso):
    chi, leaves, devices, bonds = cfg
    cols = chi * chi
    nodes = leaves - 1
    levels = devices.bit_length() - 1
    joint = min(JOINT, levels)
    span = 1 << joint
    share = chi // bonds
    items = 2 * nodes + levels + span - 1 - joint
    moves = levels - joint + 1
    f32 = jnp.float32
    dma = pltpu.SemaphoreType.DMA
    vmem = pl.BlockSpec(memory_space=pltpu.VMEM)
    hbm = pl.BlockSpec(memory_space=pl.ANY)
    packed = pl.pallas_call(
        functools.partial(kernel, cfg),
        out_shape=pltpu.VMEM((leaves + nodes + 1, chi, LANES), f32),
        in_specs=[hbm] * 3,
        out_specs=vmem,
        scratch_shapes=[
            pltpu.VMEM((1, leaves, cols), f32),
            pltpu.VMEM((bonds, devices, share, cols), f32),
            pltpu.VMEM((bonds, nodes, share, cols), f32),
            pltpu.VMEM((items, cols * chi // LANES, 2 * LANES), jnp.bfloat16),
            pltpu.VMEM((items, LANES, cols), jnp.bfloat16),
            pltpu.VMEM((items, cols * chi // LANES, 2 * LANES), jnp.bfloat16),
            pltpu.VMEM((items, 2 * LANES, cols * chi // LANES), jnp.bfloat16),
            pltpu.VMEM((4, chi, cols * chi // LANES), f32),
            pltpu.VMEM((cols, cols), jnp.bfloat16),
            pltpu.VMEM((moves, chi * chi // LANES, LANES), f32),
            pltpu.VMEM((span - 2 + moves, chi * chi // LANES, LANES), f32),
            dma((3,)),
            dma((nodes, bonds - 1)),
            dma((nodes, bonds - 1)),
            dma((span - 2 + moves,)),
            dma((span - 2 + moves,)),
            dma((moves, bonds - 1)),
            dma((moves, bonds - 1)),
            dma((span - 2 + moves,)),
            dma((span - 2 + moves,)),
        ],
        compiler_params=pltpu.CompilerParams(collective_id=0, has_side_effects=True),
        name="tree_sweep",
    )(leaf_metric, local_iso, top_iso)
    shapes = ((1, leaves, cols), (nodes, 1, cols), (1, 1, cols))
    leaf_rho, inner_rho, top_rho = pl.pallas_call(
        functools.partial(place, leaves, nodes),
        out_shape=tuple(jax.ShapeDtypeStruct(shape, f32) for shape in shapes),
        in_specs=[vmem],
        out_specs=(vmem,) * 3,
        name="place",
    )(pltpu.with_memory_space_constraint(packed, pltpu.VMEM))
    return leaf_rho, inner_rho.transpose(1, 0, 2), top_rho


def solution(mesh):
    devices, bonds = mesh.shape["leaf"], mesh.shape["bond"]
    spec = P("bond", "leaf", None)
    iso = P("leaf", "bond", None)

    def whole(leaf_metric, local_iso, top_iso):
        cfg = (local_iso.shape[1], leaf_metric.shape[1] // devices, devices, bonds)
        return jax.shard_map(
            functools.partial(body, cfg),
            mesh=mesh,
            in_specs=(spec, iso, iso),
            out_specs=(spec, spec, spec),
            check_vma=False,
        )(leaf_metric, local_iso, top_iso)

    return whole
```

```python
import functools

import jax
import jax.numpy as jnp
from jax import lax
from jax.experimental import pallas as pl
from jax.experimental.pallas import tpu as pltpu
from jax.sharding import PartitionSpec as P

LANES = 128
SUBLANES = 8
MESH = pl.DeviceIdType.MESH
EXACT = lax.Precision.HIGHEST
JOINT = 2


def mm(a, b):
    return jnp.dot(a, b, precision=EXACT, preferred_element_type=jnp.float32)


def dot(a, b):
    return jnp.dot(a, b, preferred_element_type=jnp.float32)


def dot_nt(a, b):
    return lax.dot_general(a, b, (((1,), (1,)), ((), ())), preferred_element_type=jnp.float32)


def halves(value):
    high = value.astype(jnp.bfloat16)
    low = (value - high.astype(jnp.float32)).astype(jnp.bfloat16)
    return high, low


def join_lanes(value):
    return value[:, :LANES] + value[:, LANES:]


def join_rows(value):
    half = value.shape[0] // 2
    return value[:half] + value[half:]


def kernel(
    cfg,
    leaf_hbm,
    local_hbm,
    top_hbm,
    out,
    leaf_ref,
    raw,
    loc,
    wk,
    wm,
    wq,
    yt,
    fbuf,
    perm,
    esend,
    erecv,
    own_sem,
    loc_send,
    loc_recv,
    leaf_send,
    leaf_recv,
    fwd_send,
    fwd_recv,
    env_send,
    env_recv,
):
    chi, leaves, devices, bonds = cfg
    cols = chi * chi
    rep = LANES // chi
    chunks = cols // LANES
    levels = devices.bit_length() - 1
    height_dev = leaves.bit_length() - 1
    nodes = leaves - 1
    joint = min(JOINT, levels)
    span = 1 << joint
    position = lax.axis_index("leaf")
    mine = lax.axis_index("bond")

    hops = list(range(1, span)) + [1 << k for k in range(joint, levels)]
    bits = [1 << b for b in reversed(range(bonds.bit_length() - 1))]

    barrier = pltpu.get_barrier_semaphore()
    for hop in hops:
        pl.semaphore_signal(barrier, inc=1, device_id=(position ^ hop, mine), device_id_type=MESH)
    for bit in bits:
        pl.semaphore_signal(barrier, inc=1, device_id=(position, mine ^ bit), device_id_type=MESH)
    own = [
        pltpu.make_async_copy(local_hbm, loc.at[mine], own_sem.at[0]),
        pltpu.make_async_copy(top_hbm.at[0], raw.at[mine, position], own_sem.at[1]),
        pltpu.make_async_copy(leaf_hbm, leaf_ref, own_sem.at[2]),
    ]
    for copy in own:
        copy.start()
    own[0].wait()
    own[1].wait()
    pl.semaphore_wait(barrier, len(hops) + len(bits))

    starts = [cols - (cols >> k) for k in range(levels + 1)]
    aligned = [s // LANES * LANES for s in starts]
    stops = [-(-s // LANES) * LANES for s in starts[1:-1]] + [cols]
    sends = []
    spreads = []

    class Spread:
        def __init__(self, slices, send_sem, recv_sem):
            self.copies = {}
            self.left = set(range(1, bonds))
            for d in range(1, bonds):
                bit = d & -d
                ref = slices(mine ^ (d ^ bit))
                self.copies[d] = pltpu.make_async_remote_copy(
                    src_ref=ref,
                    dst_ref=ref,
                    send_sem=send_sem.at[d - 1],
                    recv_sem=recv_sem.at[d - 1],
                    device_id=(position, mine ^ bit),
                    device_id_type=MESH,
                )

        def start(self):
            for bit in bits:
                self.copies[bit].start()
                sends.append(self.copies[bit])
            return self

        def recv(self, d):
            if d in self.left:
                self.left.remove(d)
                self.copies[d].wait_recv()

        def forward(self):
            for bit in bits:
                for d in range(1, bonds):
                    if d & -d == bit and d != bit:
                        self.recv(d ^ bit)
                        self.copies[d].start()
                        sends.append(self.copies[d])

        def finish(self):
            for d in sorted(self.left):
                self.recv(d)

    def leaf_copy(n, hop, slots):
        copy = pltpu.make_async_remote_copy(
            src_ref=slots,
            dst_ref=slots,
            send_sem=leaf_send.at[n],
            recv_sem=leaf_recv.at[n],
            device_id=(position ^ hop, mine),
            device_id_type=MESH,
        )
        copy.start()
        sends.append(copy)
        return copy

    def block(level):
        return (position >> level) << level

    local_moves = []
    for n in range(nodes):
        local_moves.append(
            Spread(lambda j, n=n: loc.at[j, n], loc_send.at[n], loc_recv.at[n]).start()
        )
    group_moves = [
        leaf_copy(hop - 1, hop, raw.at[mine, position]) for hop in reversed(range(1, span))
    ]
    far_moves = []
    top_moves = []

    def far_copy(k):
        slots = raw.at[mine, pl.ds(block(k), 1 << k), :, aligned[k] : cols]
        far_moves.append(leaf_copy(span - 1 + k - joint, 1 << k, slots))

    def top_spread(k):
        if k < joint:
            base, count, lo, hi = block(joint), span, 0, stops[joint - 1]
        else:
            base, count, lo, hi = block(k + 1), 2 << k, aligned[k], stops[k]
        n = len(top_moves)
        top_moves.append(
            Spread(
                lambda j: raw.at[j, pl.ds(base, count), :, lo:hi], fwd_send.at[n], fwd_recv.at[n]
            ).start()
        )

    own[2].wait()

    row = lax.broadcasted_iota(jnp.int32, (chi, LANES), 0)
    lane = lax.broadcasted_iota(jnp.int32, (chi, LANES), 1)
    group = lane // chi
    row_mask = group == lax.rem(row, rep)
    diag_mask = row == lane
    big_row = lax.broadcasted_iota(jnp.int32, (LANES, LANES), 0)
    big_lane = lax.broadcasted_iota(jnp.int32, (LANES, LANES), 1)
    block_mask = big_row // chi == big_lane // chi
    spread = (
        lax.broadcasted_iota(jnp.int32, (chi, chunks), 0) // rep
        == lax.broadcasted_iota(jnp.int32, (chi, chunks), 1)
    ).astype(jnp.float32)
    sub = chi // rep
    part_lane = group[:sub]
    group_lanes = [lax.rem(lane[:sub], chi) + v * chi for v in range(rep)]
    spread_lanes = [
        (lane + start) // sub for start in range(0, chi * sub, LANES)
    ]
    unit_mask = lax.rem(
        lax.broadcasted_iota(jnp.int32, (sub, chi * sub), 1), sub
    ) == lax.broadcasted_iota(jnp.int32, (sub, chi * sub), 0)
    column = lax.broadcasted_iota(jnp.int32, (chi, cols), 1)
    swapped_column = lax.broadcasted_iota(jnp.int32, (chi, cols), 0) * chi

    @pl.loop(0, chi)
    def _(a):
        perm[pl.ds(pl.multiple_of(a * chi, chi), chi), :] = (
            (column == swapped_column + a).astype(jnp.float32).astype(jnp.bfloat16)
        )

    part_group = lax.broadcasted_iota(jnp.int32, (chunks * sub, LANES), 1) // chi

    def swap_groups(value):
        parts = [
            jnp.concatenate(
                [value[g * chi + v * sub : g * chi + (v + 1) * sub] for g in range(chunks)], axis=0
            )
            for v in range(rep)
        ]
        moved = []
        for i in range(rep):
            value = parts[i]
            for v in range(rep):
                if v != i:
                    turned = pltpu.roll(parts[v], (v - i) % rep * chi, 1)
                    value = jnp.where(part_group == v, turned, value)
            moved.append(value)
        parts = moved
        return jnp.concatenate(
            [parts[v][g * sub : (g + 1) * sub] for g in range(chunks) for v in range(rep)], axis=0
        )

    def fold(value):
        terms = [value] + [pltpu.roll(value, shift, 1) for shift in range(chi, LANES, chi)]
        while len(terms) > 1:
            half = len(terms) // 2
            terms = [terms[n] + terms[n + half] for n in range(half)]
        return terms[0]

    def scaled(matrix):
        trace = jnp.sum(jnp.where(diag_mask, matrix, 0.0), axis=(0, 1), keepdims=True)
        return matrix, chi / trace

    def normal(pair):
        return pair[0] * pair[1]

    def unflatten(line):
        tile = jnp.concatenate(
            [line[:, g * LANES : (g + 1) * LANES] for g in range(chunks)], axis=0
        )
        return fold(jnp.where(row_mask, mm(spread, tile), 0.0))

    def lanes_to_rows(value):
        return jnp.concatenate(
            [value[:, g * LANES : (g + 1) * LANES] for g in range(chunks)], axis=0
        )

    def rows_to_lanes(value):
        return jnp.concatenate([value[g * chi : (g + 1) * chi] for g in range(chunks)], axis=1)

    def packed(matrix):
        value = matrix[:sub]
        for v in range(1, rep):
            value = jnp.where(part_lane == v, matrix[v * sub : (v + 1) * sub], value)
        return value

    def unpacked(value):
        return jnp.concatenate(
            [jnp.take_along_axis(value, index, axis=1) for index in group_lanes], axis=0
        )

    def stacked(value):
        return jnp.concatenate(halves(value), axis=0)

    def permute(parts):
        stack = parts[0] if len(parts) == 1 else jnp.concatenate(parts, axis=0)
        moved = dot(stack, perm[...])
        return [join_rows(moved[n * 2 * chi : (n + 1) * 2 * chi]) for n in range(len(parts))]

    def store_down(item, value):
        high, low = halves(value)
        wm[item] = jnp.concatenate([high, low] * (rep // 2), axis=0)

    def store_up(item, value):
        high, low = halves(value)
        wk[item] = jnp.concatenate([lanes_to_rows(high), lanes_to_rows(low)], axis=1)
        wq[item] = jnp.concatenate(halves(swap_groups(lanes_to_rows(value))), axis=1)

    def keep(item, acted):
        yt[item] = stacked(acted.T)

    def for_minor(env):
        block = jnp.where(block_mask, jnp.concatenate([env[0]] * rep, axis=0), 0.0)
        pair = jnp.concatenate(halves(block), axis=1)
        return jnp.concatenate([pair, pair], axis=0), env[1]

    def act_minor(item, env):
        return rows_to_lanes(join_lanes(dot(wk[item], env[0])) * env[1])

    def for_major(env):
        slot = fbuf.at[len(spreads) % fbuf.shape[0]]
        spreads.append(slot)
        slot[...] = jnp.concatenate(
            [jnp.take_along_axis(env[0], index, axis=1) for index in spread_lanes], axis=1
        )
        wide = jnp.concatenate(
            [
                jnp.where(unit_mask, jnp.broadcast_to(slot[y : y + 1, :], unit_mask.shape), 0.0)
                for y in range(chi)
            ],
            axis=0,
        )
        return jnp.concatenate(halves(wide), axis=0), env[1]

    def act_major(item, env, down=True):
        acted = dot(env[0], wq[item])
        acted = swap_groups(join_lanes(join_rows(acted)) * env[1])
        if down:
            keep(item, acted)
        return rows_to_lanes(acted)

    def close(left, right):
        high, low = halves(right)
        wide = jnp.concatenate([high] * rep + [low] * rep, axis=0)
        tall = jnp.concatenate(halves(left), axis=0)
        return scaled(join_lanes(join_rows(dot_nt(tall, wide))))

    def mix(item, state):
        state, scale = state
        high = state.astype(jnp.bfloat16).astype(jnp.float32)
        parts = jnp.where(group < rep // 2, high, state - high).astype(jnp.bfloat16)
        mixed = lanes_to_rows(dot(parts, wm[item]) * scale)
        return jnp.concatenate(halves(mixed), axis=1)

    def settle(square):
        square = join_lanes(join_rows(square))
        total = square[:chi]
        for i in range(1, rep):
            total = jnp.where(group == i, square[i * chi : (i + 1) * chi], total)
        return scaled(fold(total))

    def descend(items, mixes):
        squares = [dot(yt[item], mixed) for item, mixed in zip(items, mixes, strict=True)]
        return [settle(square) for square in squares]

    envs = [[(unflatten(leaf_ref[0, n : n + 1, :]), 1.0) for n in range(leaves)]]
    early = leaves >> 1
    for move in local_moves[:early]:
        move.forward()
    for move in group_moves:
        move.wait_recv()
    if joint < levels:
        far_copy(joint)
    top_spread(0)
    for move in local_moves[early:]:
        move.forward()

    late = []
    first = 0
    for height in range(1, height_dev + 1):
        current = envs[-1]
        count = leaves >> height
        majors = [for_major(current[2 * n]) for n in range(count)]
        minors = [for_minor(current[2 * n + 1]) for n in range(count)]
        for n in range(count):
            local_moves[first + n].finish()
        for n in range(count):
            node = first + n
            store_up(2 * node, jnp.concatenate([loc[j, node] for j in range(bonds)], axis=0))
        lefts = [act_major(2 * (first + n), majors[n], False) for n in range(count)]
        rights = [act_minor(2 * (first + n), minors[n]) for n in range(count)]
        late.extend(zip(lefts, rights, strict=True))
        grown = [close(lefts[n], rights[n]) for n in range(count)]
        envs.append(grown)
        first += count

    env = envs[-1][0]

    def env_copy(slot, n, hop):
        copy = pltpu.make_async_remote_copy(
            src_ref=esend.at[slot],
            dst_ref=erecv.at[n],
            send_sem=env_send.at[n],
            recv_sem=env_recv.at[n],
            device_id=(position ^ hop, mine),
            device_id_type=MESH,
        )
        copy.start()
        sends.append(copy)
        return copy

    def assemble(base, count, start, width):
        rows = []
        for j in range(bonds):
            rows.append(
                jnp.concatenate(
                    [raw[j, base + s, :, start : start + width] for s in range(count)], axis=1
                )
            )
        return jnp.concatenate(rows, axis=0)

    def top_value(k, r=0):
        base = ((position ^ r) >> (k + 1)) << (k + 1)
        return assemble(base, 2 << k, starts[k], cols >> (k + 1))

    def is_upper(k):
        return lax.rem(position >> k, 2) == 1

    def own_nodes(ks):
        values = [top_value(k) for k in ks]
        moved = permute([stacked(value) for value in values])
        for n, k in enumerate(ks):
            chosen = jnp.where(is_upper(k), values[n], moved[n])
            store_up(2 * nodes + k, chosen)
            store_down(2 * nodes + k, chosen)

    def local_values():
        return [
            jnp.concatenate([loc[j, node] for j in range(bonds)], axis=0) for node in range(nodes)
        ]

    esend[0] = packed(env[0])
    group_envs = [env_copy(0, hop - 1, hop) for hop in reversed(range(1, span))]

    top_moves[0].forward()
    locals_ = local_values()
    more = permute([stacked(value) for value in locals_] + [stacked(right) for _, right in late])
    for node in range(nodes):
        store_down(2 * node, locals_[node])
        store_down(2 * node + 1, more[node])
        keep(2 * node, lanes_to_rows(late[node][0]))
        keep(2 * node + 1, lanes_to_rows(more[nodes + node]))
    if joint < levels:
        far_moves[0].wait_recv()
        if joint + 1 < levels:
            far_copy(joint + 1)
        top_spread(joint)
    top_moves[0].finish()

    extra = 2 * nodes + levels
    others = {}
    tops = [top_value(k) for k in range(joint)]
    for k in range(joint):
        store_up(2 * nodes + k, tops[k])
        others[k, 0] = 2 * nodes + k
        for r in range(2 << k, span, 2 << k):
            store_up(extra, top_value(k, r))
            others[k, r] = extra
            extra += 1
    for copy in group_envs:
        copy.wait_recv()
    pool = {0: env}
    for hop in range(1, span):
        pool[hop] = scaled(unpacked(erecv[hop - 1]))
    acted = []
    for k in range(joint):
        up = is_upper(k)
        sides = {}
        for r in range(0, span, 2 << k):
            near, far = pool[r], pool[r ^ (1 << k)]
            left = [jnp.where(up, x, y) for x, y in zip(far, near, strict=True)]
            right = [jnp.where(up, x, y) for x, y in zip(near, far, strict=True)]
            sides[r] = for_major(left), for_minor(right)
        lefts = {r: act_major(others[k, r], side[0], False) for r, side in sides.items()}
        rights = {r: act_minor(others[k, r], side[1]) for r, side in sides.items()}
        following = {r: close(lefts[r], rights[r]) for r in sides}
        acted.append((lefts[0], rights[0]))
        pool = following
    env = pool[0]

    for k in range(joint, levels):
        esend[1 + k - joint] = packed(env[0])
        copy = env_copy(1 + k - joint, span - 1 + k - joint, 1 << k)
        index = k - joint + 1
        top_moves[index].forward()
        if k == joint:
            moved = permute(
                [stacked(value) for value in tops] + [stacked(right) for _, right in acted]
            )
            for n in range(joint):
                up = is_upper(n)
                store_down(2 * nodes + n, jnp.where(up, tops[n], moved[n]))
                chosen = jnp.where(up, acted[n][0], moved[joint + n])
                keep(2 * nodes + n, lanes_to_rows(chosen))
        if k + 1 < levels:
            far_moves[index].wait_recv()
            if k + 2 < levels:
                far_copy(k + 2)
            top_spread(k + 1)
        top_moves[index].finish()
        own_nodes([k])
        item = 2 * nodes + k
        minor = act_minor(item, for_minor(env))
        if k == levels - 1:
            root = assemble(0, devices, starts[levels], cols >> levels)
            state = close(root, root)
            mixed = mix(item, state)
        copy.wait_recv()
        env = close(act_major(item, for_major(scaled(unpacked(erecv[span - 1 + k - joint])))), minor)
    if joint == levels:
        root = assemble(0, devices, starts[levels], cols >> levels)
        state = close(root, root)
        mixed = mix(2 * nodes + levels - 1, state)

    top = env
    for k in range(levels - 1, -1, -1):
        marked = lax.rem(position + 1, 2 << k) == 1 << k
        top = [jnp.where(marked, x, y) for x, y in zip(state, top, strict=True)]
        (state,) = descend(
            [2 * nodes + k], [mixed if k == levels - 1 else mix(2 * nodes + k, state)]
        )
    out[leaves + nodes] = normal(top)
    states = [state]
    for height in range(height_dev, 0, -1):
        count = leaves >> height
        offset = leaves - 2 * count
        for n in range(count):
            out[leaves + offset + n] = normal(states[n])
        items = [2 * (offset + n) + 1 - side for n in range(count) for side in range(2)]
        states = descend(items, [mix(item, states[n // 2]) for n, item in enumerate(items)])
    for n in range(leaves):
        out[n] = normal(states[n])
    for copy in sends:
        copy.wait_send()


def place(leaves, nodes, packed, leaf_out, inner_out, top_out):
    chi = packed.shape[1]
    rep = LANES // chi
    row = lax.broadcasted_iota(jnp.int32, (SUBLANES, LANES), 0)
    row_mask = lax.broadcasted_iota(jnp.int32, (SUBLANES, LANES), 1) // chi == lax.rem(row, rep)
    first = 0
    for ref, count in ((leaf_out, leaves), (inner_out, nodes), (top_out, 1)):
        for n in range(count):
            for v in range(0, chi, SUBLANES):
                value = jnp.where(row_mask, packed[first + n, v : v + SUBLANES], 0.0)
                step = 1
                while step < rep:
                    value = value + pltpu.roll(value, SUBLANES - step, 0)
                    step *= 2
                for r in range(0, SUBLANES, rep):
                    g = (v + r) // rep
                    spot = (n, slice(0, 1)) if ref is inner_out else (0, slice(n, n + 1))
                    ref[spot + (slice(g * LANES, (g + 1) * LANES),)] = value[r : r + 1]
        first += count


def body(cfg, leaf_metric, local_iso, top_iso):
    chi, leaves, devices, bonds = cfg
    cols = chi * chi
    nodes = leaves - 1
    levels = devices.bit_length() - 1
    joint = min(JOINT, levels)
    span = 1 << joint
    share = chi // bonds
    items = 2 * nodes + levels + span - 1 - joint
    moves = levels - joint + 1
    f32 = jnp.float32
    dma = pltpu.SemaphoreType.DMA
    vmem = pl.BlockSpec(memory_space=pltpu.VMEM)
    hbm = pl.BlockSpec(memory_space=pl.ANY)
    packed = pl.pallas_call(
        functools.partial(kernel, cfg),
        out_shape=pltpu.VMEM((leaves + nodes + 1, chi, LANES), f32),
        in_specs=[hbm] * 3,
        out_specs=vmem,
        scratch_shapes=[
            pltpu.VMEM((1, leaves, cols), f32),
            pltpu.VMEM((bonds, devices, share, cols), f32),
            pltpu.VMEM((bonds, nodes, share, cols), f32),
            pltpu.VMEM((items, cols * chi // LANES, 2 * LANES), jnp.bfloat16),
            pltpu.VMEM((items, LANES, cols), jnp.bfloat16),
            pltpu.VMEM((items, cols * chi // LANES, 2 * LANES), jnp.bfloat16),
            pltpu.VMEM((items, 2 * LANES, cols * chi // LANES), jnp.bfloat16),
            pltpu.VMEM((4, chi, cols * chi // LANES), f32),
            pltpu.VMEM((cols, cols), jnp.bfloat16),
            pltpu.VMEM((moves, chi * chi // LANES, LANES), f32),
            pltpu.VMEM((span - 2 + moves, chi * chi // LANES, LANES), f32),
            dma((3,)),
            dma((nodes, bonds - 1)),
            dma((nodes, bonds - 1)),
            dma((span - 2 + moves,)),
            dma((span - 2 + moves,)),
            dma((moves, bonds - 1)),
            dma((moves, bonds - 1)),
            dma((span - 2 + moves,)),
            dma((span - 2 + moves,)),
        ],
        compiler_params=pltpu.CompilerParams(collective_id=0, has_side_effects=True),
        name="tree_sweep",
    )(leaf_metric, local_iso, top_iso)
    shapes = ((1, leaves, cols), (nodes, 1, cols), (1, 1, cols))
    leaf_rho, inner_rho, top_rho = pl.pallas_call(
        functools.partial(place, leaves, nodes),
        out_shape=tuple(jax.ShapeDtypeStruct(shape, f32) for shape in shapes),
        in_specs=[vmem],
        out_specs=(vmem,) * 3,
        name="place",
    )(pltpu.with_memory_space_constraint(packed, pltpu.VMEM))
    return leaf_rho, inner_rho.transpose(1, 0, 2), top_rho


def solution(mesh):
    devices, bonds = mesh.shape["leaf"], mesh.shape["bond"]
    spec = P("bond", "leaf", None)
    iso = P("leaf", "bond", None)

    def whole(leaf_metric, local_iso, top_iso):
        cfg = (local_iso.shape[1], leaf_metric.shape[1] // devices, devices, bonds)
        return jax.shard_map(
            functools.partial(body, cfg),
            mesh=mesh,
            in_specs=(spec, iso, iso),
            out_specs=(spec, spec, spec),
            check_vma=False,
        )(leaf_metric, local_iso, top_iso)

    return whole
```

```python
import functools

import jax
import jax.numpy as jnp
from jax import lax
from jax.experimental import pallas as pl
from jax.experimental.pallas import tpu as pltpu
from jax.sharding import PartitionSpec as P

LANES = 128
SUBLANES = 8
MESH = pl.DeviceIdType.MESH
EXACT = lax.Precision.HIGHEST
JOINT = 2


def mm(a, b):
    return jnp.dot(a, b, precision=EXACT, preferred_element_type=jnp.float32)


def dot(a, b):
    return jnp.dot(a, b, preferred_element_type=jnp.float32)


def dot_nt(a, b):
    return lax.dot_general(a, b, (((1,), (1,)), ((), ())), preferred_element_type=jnp.float32)


def halves(value):
    high = value.astype(jnp.bfloat16)
    low = (value - high.astype(jnp.float32)).astype(jnp.bfloat16)
    return high, low


def join_lanes(value):
    return value[:, :LANES] + value[:, LANES:]


def join_rows(value):
    half = value.shape[0] // 2
    return value[:half] + value[half:]


def kernel(
    cfg,
    leaf_hbm,
    local_hbm,
    top_hbm,
    out,
    leaf_ref,
    raw,
    loc,
    wk,
    wm,
    wq,
    yt,
    fbuf,
    perm,
    esend,
    erecv,
    own_sem,
    loc_send,
    loc_recv,
    leaf_send,
    leaf_recv,
    fwd_send,
    fwd_recv,
    env_send,
    env_recv,
):
    chi, leaves, devices, bonds = cfg
    cols = chi * chi
    rep = LANES // chi
    chunks = cols // LANES
    levels = devices.bit_length() - 1
    height_dev = leaves.bit_length() - 1
    nodes = leaves - 1
    joint = min(JOINT, levels)
    span = 1 << joint
    position = lax.axis_index("leaf")
    mine = lax.axis_index("bond")

    hops = list(range(1, span)) + [1 << k for k in range(joint, levels)]
    bits = [1 << b for b in reversed(range(bonds.bit_length() - 1))]

    barrier = pltpu.get_barrier_semaphore()
    for hop in hops:
        pl.semaphore_signal(barrier, inc=1, device_id=(position ^ hop, mine), device_id_type=MESH)
    for bit in bits:
        pl.semaphore_signal(barrier, inc=1, device_id=(position, mine ^ bit), device_id_type=MESH)
    own = [
        pltpu.make_async_copy(local_hbm, loc.at[mine], own_sem.at[0]),
        pltpu.make_async_copy(top_hbm.at[0], raw.at[mine, position], own_sem.at[1]),
        pltpu.make_async_copy(leaf_hbm, leaf_ref, own_sem.at[2]),
    ]
    for copy in own:
        copy.start()
    own[0].wait()
    own[1].wait()
    pl.semaphore_wait(barrier, len(hops) + len(bits))

    starts = [cols - (cols >> k) for k in range(levels + 1)]
    aligned = [s // LANES * LANES for s in starts]
    stops = [-(-s // LANES) * LANES for s in starts[1:-1]] + [cols]
    sends = []
    spreads = []

    class Spread:
        def __init__(self, slices, send_sem, recv_sem):
            self.copies = {}
            self.left = set(range(1, bonds))
            for d in range(1, bonds):
                bit = d & -d
                ref = slices(mine ^ (d ^ bit))
                self.copies[d] = pltpu.make_async_remote_copy(
                    src_ref=ref,
                    dst_ref=ref,
                    send_sem=send_sem.at[d - 1],
                    recv_sem=recv_sem.at[d - 1],
                    device_id=(position, mine ^ bit),
                    device_id_type=MESH,
                )

        def start(self):
            for bit in bits:
                self.copies[bit].start()
                sends.append(self.copies[bit])
            return self

        def recv(self, d):
            if d in self.left:
                self.left.remove(d)
                self.copies[d].wait_recv()

        def forward(self):
            for bit in bits:
                for d in range(1, bonds):
                    if d & -d == bit and d != bit:
                        self.recv(d ^ bit)
                        self.copies[d].start()
                        sends.append(self.copies[d])

        def finish(self):
            for d in sorted(self.left):
                self.recv(d)

    def leaf_copy(n, hop, slots):
        copy = pltpu.make_async_remote_copy(
            src_ref=slots,
            dst_ref=slots,
            send_sem=leaf_send.at[n],
            recv_sem=leaf_recv.at[n],
            device_id=(position ^ hop, mine),
            device_id_type=MESH,
        )
        copy.start()
        sends.append(copy)
        return copy

    def block(level):
        return (position >> level) << level

    local_moves = []
    for n in range(nodes):
        local_moves.append(
            Spread(lambda j, n=n: loc.at[j, n], loc_send.at[n], loc_recv.at[n]).start()
        )
    group_moves = [
        leaf_copy(hop - 1, hop, raw.at[mine, position]) for hop in reversed(range(1, span))
    ]
    far_moves = []
    top_moves = []

    def far_copy(k):
        slots = raw.at[mine, pl.ds(block(k), 1 << k), :, aligned[k] : cols]
        far_moves.append(leaf_copy(span - 1 + k - joint, 1 << k, slots))

    def top_spread(k):
        if k < joint:
            base, count, lo, hi = block(joint), span, 0, stops[joint - 1]
        else:
            base, count, lo, hi = block(k + 1), 2 << k, aligned[k], stops[k]
        n = len(top_moves)
        top_moves.append(
            Spread(
                lambda j: raw.at[j, pl.ds(base, count), :, lo:hi], fwd_send.at[n], fwd_recv.at[n]
            ).start()
        )

    own[2].wait()

    row = lax.broadcasted_iota(jnp.int32, (chi, LANES), 0)
    lane = lax.broadcasted_iota(jnp.int32, (chi, LANES), 1)
    group = lane // chi
    row_mask = group == lax.rem(row, rep)
    diag_mask = row == lane
    spread = (
        lax.broadcasted_iota(jnp.int32, (chi, chunks), 0) // rep
        == lax.broadcasted_iota(jnp.int32, (chi, chunks), 1)
    ).astype(jnp.float32)
    sub = chi // rep
    part_lane = group[:sub]
    group_lanes = [lax.rem(lane[:sub], chi) + v * chi for v in range(rep)]
    spread_lanes = [
        (lane + start) // sub for start in range(0, chi * sub, LANES)
    ]
    unit_mask = lax.rem(
        lax.broadcasted_iota(jnp.int32, (sub, chi * sub), 1), sub
    ) == lax.broadcasted_iota(jnp.int32, (sub, chi * sub), 0)
    column = lax.broadcasted_iota(jnp.int32, (chi, cols), 1)
    swapped_column = lax.broadcasted_iota(jnp.int32, (chi, cols), 0) * chi

    @pl.loop(0, chi)
    def _(a):
        perm[pl.ds(pl.multiple_of(a * chi, chi), chi), :] = (
            (column == swapped_column + a).astype(jnp.float32).astype(jnp.bfloat16)
        )

    part_group = lax.broadcasted_iota(jnp.int32, (chunks * sub, LANES), 1) // chi

    def swap_groups(value):
        parts = [
            jnp.concatenate(
                [value[g * chi + v * sub : g * chi + (v + 1) * sub] for g in range(chunks)], axis=0
            )
            for v in range(rep)
        ]
        moved = []
        for i in range(rep):
            value = parts[i]
            for v in range(rep):
                if v != i:
                    turned = pltpu.roll(parts[v], (v - i) % rep * chi, 1)
                    value = jnp.where(part_group == v, turned, value)
            moved.append(value)
        parts = moved
        return jnp.concatenate(
            [parts[v][g * sub : (g + 1) * sub] for g in range(chunks) for v in range(rep)], axis=0
        )

    def fold(value):
        terms = [value] + [pltpu.roll(value, shift, 1) for shift in range(chi, LANES, chi)]
        while len(terms) > 1:
            half = len(terms) // 2
            terms = [terms[n] + terms[n + half] for n in range(half)]
        return terms[0]

    def scaled(matrix):
        trace = jnp.sum(jnp.where(diag_mask, matrix, 0.0), axis=(0, 1), keepdims=True)
        return matrix, chi / trace

    def normal(pair):
        return pair[0] * pair[1]

    def unflatten(line):
        tile = jnp.concatenate(
            [line[:, g * LANES : (g + 1) * LANES] for g in range(chunks)], axis=0
        )
        return fold(jnp.where(row_mask, mm(spread, tile), 0.0))

    def lanes_to_rows(value):
        return jnp.concatenate(
            [value[:, g * LANES : (g + 1) * LANES] for g in range(chunks)], axis=0
        )

    def rows_to_lanes(value):
        return jnp.concatenate([value[g * chi : (g + 1) * chi] for g in range(chunks)], axis=1)

    def packed(matrix):
        value = matrix[:sub]
        for v in range(1, rep):
            value = jnp.where(part_lane == v, matrix[v * sub : (v + 1) * sub], value)
        return value

    def unpacked(value):
        return jnp.concatenate(
            [jnp.take_along_axis(value, index, axis=1) for index in group_lanes], axis=0
        )

    def stacked(value):
        return jnp.concatenate(halves(value), axis=0)

    def permute(parts):
        stack = parts[0] if len(parts) == 1 else jnp.concatenate(parts, axis=0)
        moved = dot(stack, perm[...])
        return [join_rows(moved[n * 2 * chi : (n + 1) * 2 * chi]) for n in range(len(parts))]

    def store_down(item, value):
        high, low = halves(value)
        wm[item] = jnp.concatenate([high, low] * (rep // 2), axis=0)

    def store_up(item, value):
        high, low = halves(value)
        wk[item] = jnp.concatenate([lanes_to_rows(high), lanes_to_rows(low)], axis=1)
        wq[item] = jnp.concatenate(halves(swap_groups(lanes_to_rows(value))), axis=1)

    def keep(item, acted):
        yt[item] = stacked(acted.T)

    def for_minor(env):
        block = jnp.concatenate([jnp.where(group == i, env[0], 0.0) for i in range(rep)], axis=0)
        pair = jnp.concatenate(halves(block), axis=1)
        return jnp.concatenate([pair, pair], axis=0), env[1]

    def act_minor(item, env):
        return rows_to_lanes(join_lanes(dot(wk[item], env[0])) * env[1])

    def for_major(env):
        slot = fbuf.at[len(spreads) % fbuf.shape[0]]
        spreads.append(slot)
        slot[...] = jnp.concatenate(
            [jnp.take_along_axis(env[0], index, axis=1) for index in spread_lanes], axis=1
        )
        wide = jnp.concatenate(
            [
                jnp.where(unit_mask, jnp.broadcast_to(slot[y : y + 1, :], unit_mask.shape), 0.0)
                for y in range(chi)
            ],
            axis=0,
        )
        return jnp.concatenate(halves(wide), axis=0), env[1]

    def act_major(item, env, down=True):
        acted = dot(env[0], wq[item])
        acted = swap_groups(join_lanes(join_rows(acted)) * env[1])
        if down:
            keep(item, acted)
        return rows_to_lanes(acted)

    def close(left, right):
        high, low = halves(right)
        wide = jnp.concatenate([high] * rep + [low] * rep, axis=0)
        tall = jnp.concatenate(halves(left), axis=0)
        return scaled(join_lanes(join_rows(dot_nt(tall, wide))))

    def mix(item, state):
        state, scale = state
        high = state.astype(jnp.bfloat16).astype(jnp.float32)
        parts = jnp.where(group < rep // 2, high, state - high).astype(jnp.bfloat16)
        return lanes_to_rows(dot(parts, wm[item]) * scale)

    def settle(square):
        square = join_lanes(join_rows(square))
        total = square[:chi]
        for i in range(1, rep):
            total = jnp.where(group == i, square[i * chi : (i + 1) * chi], total)
        return scaled(fold(total))

    def descend(items, mixes):
        squares = [
            dot(yt[item], jnp.concatenate(halves(mixed), axis=1))
            for item, mixed in zip(items, mixes, strict=True)
        ]
        return [settle(square) for square in squares]

    envs = [[(unflatten(leaf_ref[0, n : n + 1, :]), 1.0) for n in range(leaves)]]
    early = leaves >> 1
    for move in local_moves[:early]:
        move.forward()
    for move in group_moves:
        move.wait_recv()
    if joint < levels:
        far_copy(joint)
    top_spread(0)
    for move in local_moves[early:]:
        move.forward()

    late = []
    first = 0
    for height in range(1, height_dev + 1):
        current = envs[-1]
        count = leaves >> height
        majors = [for_major(current[2 * n]) for n in range(count)]
        minors = [for_minor(current[2 * n + 1]) for n in range(count)]
        for n in range(count):
            local_moves[first + n].finish()
        for n in range(count):
            node = first + n
            store_up(2 * node, jnp.concatenate([loc[j, node] for j in range(bonds)], axis=0))
        lefts = [act_major(2 * (first + n), majors[n], False) for n in range(count)]
        rights = [act_minor(2 * (first + n), minors[n]) for n in range(count)]
        late.extend(zip(lefts, rights, strict=True))
        grown = [close(lefts[n], rights[n]) for n in range(count)]
        envs.append(grown)
        first += count

    env = envs[-1][0]

    def env_copy(slot, n, hop):
        copy = pltpu.make_async_remote_copy(
            src_ref=esend.at[slot],
            dst_ref=erecv.at[n],
            send_sem=env_send.at[n],
            recv_sem=env_recv.at[n],
            device_id=(position ^ hop, mine),
            device_id_type=MESH,
        )
        copy.start()
        sends.append(copy)
        return copy

    def assemble(base, count, start, width):
        rows = []
        for j in range(bonds):
            rows.append(
                jnp.concatenate(
                    [raw[j, base + s, :, start : start + width] for s in range(count)], axis=1
                )
            )
        return jnp.concatenate(rows, axis=0)

    def top_value(k, r=0):
        base = ((position ^ r) >> (k + 1)) << (k + 1)
        return assemble(base, 2 << k, starts[k], cols >> (k + 1))

    def is_upper(k):
        return lax.rem(position >> k, 2) == 1

    def own_nodes(ks):
        values = [top_value(k) for k in ks]
        moved = permute([stacked(value) for value in values])
        for n, k in enumerate(ks):
            chosen = jnp.where(is_upper(k), values[n], moved[n])
            store_up(2 * nodes + k, chosen)
            store_down(2 * nodes + k, chosen)

    def local_values():
        return [
            jnp.concatenate([loc[j, node] for j in range(bonds)], axis=0) for node in range(nodes)
        ]

    esend[0] = packed(env[0])
    group_envs = [env_copy(0, hop - 1, hop) for hop in reversed(range(1, span))]

    top_moves[0].forward()
    locals_ = local_values()
    more = permute([stacked(value) for value in locals_] + [stacked(right) for _, right in late])
    for node in range(nodes):
        store_down(2 * node, locals_[node])
        store_down(2 * node + 1, more[node])
        keep(2 * node, lanes_to_rows(late[node][0]))
        keep(2 * node + 1, lanes_to_rows(more[nodes + node]))
    if joint < levels:
        far_moves[0].wait_recv()
        if joint + 1 < levels:
            far_copy(joint + 1)
        top_spread(joint)
    top_moves[0].finish()

    extra = 2 * nodes + levels
    others = {}
    tops = [top_value(k) for k in range(joint)]
    for k in range(joint):
        store_up(2 * nodes + k, tops[k])
        others[k, 0] = 2 * nodes + k
        for r in range(2 << k, span, 2 << k):
            store_up(extra, top_value(k, r))
            others[k, r] = extra
            extra += 1
    for copy in group_envs:
        copy.wait_recv()
    pool = {0: env}
    for hop in range(1, span):
        pool[hop] = scaled(unpacked(erecv[hop - 1]))
    acted = []
    for k in range(joint):
        up = is_upper(k)
        sides = {}
        for r in range(0, span, 2 << k):
            near, far = pool[r], pool[r ^ (1 << k)]
            left = [jnp.where(up, x, y) for x, y in zip(far, near, strict=True)]
            right = [jnp.where(up, x, y) for x, y in zip(near, far, strict=True)]
            sides[r] = for_major(left), for_minor(right)
        lefts = {r: act_major(others[k, r], side[0], False) for r, side in sides.items()}
        rights = {r: act_minor(others[k, r], side[1]) for r, side in sides.items()}
        following = {r: close(lefts[r], rights[r]) for r in sides}
        acted.append((lefts[0], rights[0]))
        pool = following
    env = pool[0]

    for k in range(joint, levels):
        esend[1 + k - joint] = packed(env[0])
        copy = env_copy(1 + k - joint, span - 1 + k - joint, 1 << k)
        index = k - joint + 1
        top_moves[index].forward()
        if k == joint:
            moved = permute(
                [stacked(value) for value in tops] + [stacked(right) for _, right in acted]
            )
            for n in range(joint):
                up = is_upper(n)
                store_down(2 * nodes + n, jnp.where(up, tops[n], moved[n]))
                chosen = jnp.where(up, acted[n][0], moved[joint + n])
                keep(2 * nodes + n, lanes_to_rows(chosen))
        if k + 1 < levels:
            far_moves[index].wait_recv()
            if k + 2 < levels:
                far_copy(k + 2)
            top_spread(k + 1)
        top_moves[index].finish()
        own_nodes([k])
        item = 2 * nodes + k
        minor = act_minor(item, for_minor(env))
        if k == levels - 1:
            root = assemble(0, devices, starts[levels], cols >> levels)
            state = close(root, root)
            keep(item, mix(item, state))
        copy.wait_recv()
        last = k == levels - 1
        major = act_major(item, for_major(scaled(unpacked(erecv[span - 1 + k - joint]))), not last)
        env = close(major, minor)
    if joint == levels:
        root = assemble(0, devices, starts[levels], cols >> levels)
        state = close(root, root)
        mixed = mix(2 * nodes + levels - 1, state)

    top = env
    for k in range(levels - 1, -1, -1):
        marked = lax.rem(position + 1, 2 << k) == 1 << k
        top = [jnp.where(marked, x, y) for x, y in zip(state, top, strict=True)]
        mixed = lanes_to_rows(major) if k == levels - 1 else mix(2 * nodes + k, state)
        (state,) = descend([2 * nodes + k], [mixed])
    out[leaves + nodes] = normal(top)
    states = [state]
    for height in range(height_dev, 0, -1):
        count = leaves >> height
        offset = leaves - 2 * count
        for n in range(count):
            out[leaves + offset + n] = normal(states[n])
        items = [2 * (offset + n) + 1 - side for n in range(count) for side in range(2)]
        states = descend(items, [mix(item, states[n // 2]) for n, item in enumerate(items)])
    for n in range(leaves):
        out[n] = normal(states[n])
    for copy in sends:
        copy.wait_send()


def place(leaves, nodes, packed, leaf_out, inner_out, top_out):
    chi = packed.shape[1]
    rep = LANES // chi
    row = lax.broadcasted_iota(jnp.int32, (SUBLANES, LANES), 0)
    row_mask = lax.broadcasted_iota(jnp.int32, (SUBLANES, LANES), 1) // chi == lax.rem(row, rep)
    first = 0
    for ref, count in ((leaf_out, leaves), (inner_out, nodes), (top_out, 1)):
        for n in range(count):
            for v in range(0, chi, SUBLANES):
                value = jnp.where(row_mask, packed[first + n, v : v + SUBLANES], 0.0)
                step = 1
                while step < rep:
                    value = value + pltpu.roll(value, SUBLANES - step, 0)
                    step *= 2
                for r in range(0, SUBLANES, rep):
                    g = (v + r) // rep
                    spot = (n, slice(0, 1)) if ref is inner_out else (0, slice(n, n + 1))
                    ref[spot + (slice(g * LANES, (g + 1) * LANES),)] = value[r : r + 1]
        first += count


def body(cfg, leaf_metric, local_iso, top_iso):
    chi, leaves, devices, bonds = cfg
    cols = chi * chi
    nodes = leaves - 1
    levels = devices.bit_length() - 1
    joint = min(JOINT, levels)
    span = 1 << joint
    share = chi // bonds
    items = 2 * nodes + levels + span - 1 - joint
    moves = levels - joint + 1
    f32 = jnp.float32
    dma = pltpu.SemaphoreType.DMA
    vmem = pl.BlockSpec(memory_space=pltpu.VMEM)
    hbm = pl.BlockSpec(memory_space=pl.ANY)
    packed = pl.pallas_call(
        functools.partial(kernel, cfg),
        out_shape=pltpu.VMEM((leaves + nodes + 1, chi, LANES), f32),
        in_specs=[hbm] * 3,
        out_specs=vmem,
        scratch_shapes=[
            pltpu.VMEM((1, leaves, cols), f32),
            pltpu.VMEM((bonds, devices, share, cols), f32),
            pltpu.VMEM((bonds, nodes, share, cols), f32),
            pltpu.VMEM((items, cols * chi // LANES, 2 * LANES), jnp.bfloat16),
            pltpu.VMEM((items, LANES, cols), jnp.bfloat16),
            pltpu.VMEM((items, cols * chi // LANES, 2 * LANES), jnp.bfloat16),
            pltpu.VMEM((items, 2 * LANES, cols * chi // LANES), jnp.bfloat16),
            pltpu.VMEM((4, chi, cols * chi // LANES), f32),
            pltpu.VMEM((cols, cols), jnp.bfloat16),
            pltpu.VMEM((moves, chi * chi // LANES, LANES), f32),
            pltpu.VMEM((span - 2 + moves, chi * chi // LANES, LANES), f32),
            dma((3,)),
            dma((nodes, bonds - 1)),
            dma((nodes, bonds - 1)),
            dma((span - 2 + moves,)),
            dma((span - 2 + moves,)),
            dma((moves, bonds - 1)),
            dma((moves, bonds - 1)),
            dma((span - 2 + moves,)),
            dma((span - 2 + moves,)),
        ],
        compiler_params=pltpu.CompilerParams(collective_id=0, has_side_effects=True),
        name="tree_sweep",
    )(leaf_metric, local_iso, top_iso)
    shapes = ((1, leaves, cols), (nodes, 1, cols), (1, 1, cols))
    leaf_rho, inner_rho, top_rho = pl.pallas_call(
        functools.partial(place, leaves, nodes),
        out_shape=tuple(jax.ShapeDtypeStruct(shape, f32) for shape in shapes),
        in_specs=[vmem],
        out_specs=(vmem,) * 3,
        name="place",
    )(pltpu.with_memory_space_constraint(packed, pltpu.VMEM))
    return leaf_rho, inner_rho.transpose(1, 0, 2), top_rho


def solution(mesh):
    devices, bonds = mesh.shape["leaf"], mesh.shape["bond"]
    spec = P("bond", "leaf", None)
    iso = P("leaf", "bond", None)

    def whole(leaf_metric, local_iso, top_iso):
        cfg = (local_iso.shape[1], leaf_metric.shape[1] // devices, devices, bonds)
        return jax.shard_map(
            functools.partial(body, cfg),
            mesh=mesh,
            in_specs=(spec, iso, iso),
            out_specs=(spec, spec, spec),
            check_vma=False,
        )(leaf_metric, local_iso, top_iso)

    return whole
```

```python
import functools

import jax
import jax.numpy as jnp
from jax import lax
from jax.experimental import pallas as pl
from jax.experimental.pallas import tpu as pltpu
from jax.sharding import PartitionSpec as P

LANES = 128
SUBLANES = 8
MESH = pl.DeviceIdType.MESH
EXACT = lax.Precision.HIGHEST
JOINT = 2


def mm(a, b):
    return jnp.dot(a, b, precision=EXACT, preferred_element_type=jnp.float32)


def dot(a, b):
    return jnp.dot(a, b, preferred_element_type=jnp.float32)


def dot_nt(a, b):
    return lax.dot_general(a, b, (((1,), (1,)), ((), ())), preferred_element_type=jnp.float32)


def halves(value):
    high = value.astype(jnp.bfloat16)
    low = (value - high.astype(jnp.float32)).astype(jnp.bfloat16)
    return high, low


def join_lanes(value):
    return value[:, :LANES] + value[:, LANES:]


def join_rows(value):
    half = value.shape[0] // 2
    return value[:half] + value[half:]


def kernel(
    cfg,
    leaf_hbm,
    local_hbm,
    top_hbm,
    out,
    leaf_ref,
    raw,
    loc,
    wk,
    wm,
    wq,
    yt,
    fbuf,
    perm,
    esend,
    erecv,
    own_sem,
    loc_send,
    loc_recv,
    leaf_send,
    leaf_recv,
    fwd_send,
    fwd_recv,
    env_send,
    env_recv,
):
    chi, leaves, devices, bonds = cfg
    cols = chi * chi
    rep = LANES // chi
    chunks = cols // LANES
    levels = devices.bit_length() - 1
    height_dev = leaves.bit_length() - 1
    nodes = leaves - 1
    joint = min(JOINT, levels)
    span = 1 << joint
    position = lax.axis_index("leaf")
    mine = lax.axis_index("bond")

    hops = list(range(1, span)) + [1 << k for k in range(joint, levels)]
    bits = [1 << b for b in reversed(range(bonds.bit_length() - 1))]

    barrier = pltpu.get_barrier_semaphore()
    for hop in hops:
        pl.semaphore_signal(barrier, inc=1, device_id=(position ^ hop, mine), device_id_type=MESH)
    for bit in range(1, bonds):
        pl.semaphore_signal(barrier, inc=1, device_id=(position, mine ^ bit), device_id_type=MESH)
    own = [
        pltpu.make_async_copy(local_hbm, loc.at[mine], own_sem.at[0]),
        pltpu.make_async_copy(top_hbm.at[0], raw.at[mine, position], own_sem.at[1]),
        pltpu.make_async_copy(leaf_hbm, leaf_ref, own_sem.at[2]),
    ]
    for copy in own:
        copy.start()
    own[0].wait()
    own[1].wait()
    pl.semaphore_wait(barrier, len(hops) + bonds - 1)

    starts = [cols - (cols >> k) for k in range(levels + 1)]
    aligned = [s // LANES * LANES for s in starts]
    stops = [-(-s // LANES) * LANES for s in starts[1:-1]] + [cols]
    sends = []
    spreads = []

    class Spread:
        def __init__(self, slices, send_sem, recv_sem, direct=False):
            self.copies = {}
            self.direct = direct
            self.left = set(range(1, bonds))
            for d in range(1, bonds):
                bit = d if direct else d & -d
                ref = slices(mine ^ (d ^ bit))
                self.copies[d] = pltpu.make_async_remote_copy(
                    src_ref=ref,
                    dst_ref=ref,
                    send_sem=send_sem.at[d - 1],
                    recv_sem=recv_sem.at[d - 1],
                    device_id=(position, mine ^ bit),
                    device_id_type=MESH,
                )

        def start(self):
            for bit in reversed(range(1, bonds)) if self.direct else bits:
                self.copies[bit].start()
                sends.append(self.copies[bit])
            return self

        def sent(self):
            for bit in bits[:-1]:
                self.copies[bit].wait_send()
                del sends[next(n for n, c in enumerate(sends) if c is self.copies[bit])]

        def recv(self, d):
            if d in self.left:
                self.left.remove(d)
                self.copies[d].wait_recv()

        def forward(self):
            for bit in bits:
                for d in range(1, bonds):
                    if d & -d == bit and d != bit and not self.direct:
                        self.recv(d ^ bit)
                        self.copies[d].start()
                        sends.append(self.copies[d])

        def finish(self):
            for d in sorted(self.left):
                self.recv(d)

    def leaf_copy(n, hop, slots):
        copy = pltpu.make_async_remote_copy(
            src_ref=slots,
            dst_ref=slots,
            send_sem=leaf_send.at[n],
            recv_sem=leaf_recv.at[n],
            device_id=(position ^ hop, mine),
            device_id_type=MESH,
        )
        copy.start()
        sends.append(copy)
        return copy

    def block(level):
        return (position >> level) << level

    early = leaves >> 1
    local_moves = [
        Spread(lambda j, n=n: loc.at[j, n], loc_send.at[n], loc_recv.at[n], n >= early) for n in range(nodes)
    ]
    for move in local_moves[:early]:
        move.start()
    group_moves = [
        leaf_copy(hop - 1, hop, raw.at[mine, position]) for hop in reversed(range(1, span))
    ]
    for move in local_moves[early:]:
        move.start()
    far_moves = []
    top_moves = []

    def far_copy(k):
        slots = raw.at[mine, pl.ds(block(k), 1 << k), :, aligned[k] : cols]
        far_moves.append(leaf_copy(span - 1 + k - joint, 1 << k, slots))

    def top_spread(k):
        if k < joint:
            base, count, lo, hi = block(joint), span, 0, stops[joint - 1]
        else:
            base, count, lo, hi = block(k + 1), 2 << k, aligned[k], stops[k]
        n = len(top_moves)
        top_moves.append(
            Spread(
                lambda j: raw.at[j, pl.ds(base, count), :, lo:hi], fwd_send.at[n], fwd_recv.at[n]
            ).start()
        )

    own[2].wait()

    row = lax.broadcasted_iota(jnp.int32, (chi, LANES), 0)
    lane = lax.broadcasted_iota(jnp.int32, (chi, LANES), 1)
    group = lane // chi
    row_mask = group == lax.rem(row, rep)
    diag_mask = row == lane
    unfolded_mask = row == lax.rem(lane, chi)
    spread = (
        lax.broadcasted_iota(jnp.int32, (chi, chunks), 0) // rep
        == lax.broadcasted_iota(jnp.int32, (chi, chunks), 1)
    ).astype(jnp.float32)
    sub = chi // rep
    part_lane = group[:sub]
    group_lanes = [lax.rem(lane[:sub], chi) + v * chi for v in range(rep)]
    spread_lanes = [
        (lane + start) // sub for start in range(0, chi * sub, LANES)
    ]
    unit_mask = lax.rem(
        lax.broadcasted_iota(jnp.int32, (sub, chi * sub), 1), sub
    ) == lax.broadcasted_iota(jnp.int32, (sub, chi * sub), 0)
    column = lax.broadcasted_iota(jnp.int32, (chi, cols), 1)
    swapped_column = lax.broadcasted_iota(jnp.int32, (chi, cols), 0) * chi

    @pl.loop(0, chi)
    def _(a):
        perm[pl.ds(pl.multiple_of(a * chi, chi), chi), :] = (
            (column == swapped_column + a).astype(jnp.float32).astype(jnp.bfloat16)
        )

    part_group = lax.broadcasted_iota(jnp.int32, (chunks * sub, LANES), 1) // chi

    def swap_groups(value):
        parts = [
            jnp.concatenate(
                [value[g * chi + v * sub : g * chi + (v + 1) * sub] for g in range(chunks)], axis=0
            )
            for v in range(rep)
        ]
        moved = []
        for i in range(rep):
            value = parts[i]
            for v in range(rep):
                if v != i:
                    turned = pltpu.roll(parts[v], (v - i) % rep * chi, 1)
                    value = jnp.where(part_group == v, turned, value)
            moved.append(value)
        parts = moved
        return jnp.concatenate(
            [parts[v][g * sub : (g + 1) * sub] for g in range(chunks) for v in range(rep)], axis=0
        )

    def fold(value):
        terms = [value] + [pltpu.roll(value, shift, 1) for shift in range(chi, LANES, chi)]
        while len(terms) > 1:
            half = len(terms) // 2
            terms = [terms[n] + terms[n + half] for n in range(half)]
        return terms[0]

    def scaled(matrix, mask=None):
        mask = diag_mask if mask is None else mask
        trace = jnp.sum(jnp.where(mask, matrix, 0.0), axis=(0, 1), keepdims=True)
        return matrix, chi / trace

    def normal(pair):
        return fold(pair[0]) * pair[1]

    def unflatten(line):
        tile = jnp.concatenate(
            [line[:, g * LANES : (g + 1) * LANES] for g in range(chunks)], axis=0
        )
        return fold(jnp.where(row_mask, mm(spread, tile), 0.0))

    def lanes_to_rows(value):
        return jnp.concatenate(
            [value[:, g * LANES : (g + 1) * LANES] for g in range(chunks)], axis=0
        )

    def rows_to_lanes(value):
        return jnp.concatenate([value[g * chi : (g + 1) * chi] for g in range(chunks)], axis=1)

    def packed(matrix):
        value = matrix[:sub]
        for v in range(1, rep):
            value = jnp.where(part_lane == v, matrix[v * sub : (v + 1) * sub], value)
        return value

    def unpacked(value):
        return jnp.concatenate(
            [jnp.take_along_axis(value, index, axis=1) for index in group_lanes], axis=0
        )

    def stacked(value):
        return jnp.concatenate(halves(value), axis=0)

    def permute(parts):
        stack = parts[0] if len(parts) == 1 else jnp.concatenate(parts, axis=0)
        moved = dot(stack, perm[...])
        return [join_rows(moved[n * 2 * chi : (n + 1) * 2 * chi]) for n in range(len(parts))]

    def store_down(item, value):
        high, low = halves(value)
        wm[item] = jnp.concatenate([high] * rep + [low] * rep, axis=0)

    def store_up(item, value):
        high, low = halves(value)
        wk[item] = jnp.concatenate([lanes_to_rows(high), lanes_to_rows(low)], axis=1)
        wq[item] = jnp.concatenate(halves(swap_groups(lanes_to_rows(value))), axis=1)

    def keep(item, acted):
        yt[item] = stacked(acted.T)

    def for_minor(env):
        block = jnp.concatenate([jnp.where(group == i, env[0], 0.0) for i in range(rep)], axis=0)
        pair = jnp.concatenate(halves(block), axis=1)
        return jnp.concatenate([pair, pair], axis=0), env[1]

    def act_minor(item, env):
        return rows_to_lanes(join_lanes(dot(wk[item], env[0])) * env[1])

    def for_major(env):
        slot = fbuf.at[len(spreads) % fbuf.shape[0]]
        spreads.append(slot)
        slot[...] = jnp.concatenate(
            [jnp.take_along_axis(env[0], index, axis=1) for index in spread_lanes], axis=1
        )
        wide = jnp.concatenate(
            [
                jnp.where(unit_mask, jnp.broadcast_to(slot[y : y + 1, :], unit_mask.shape), 0.0)
                for y in range(chi)
            ],
            axis=0,
        )
        return jnp.concatenate(halves(wide), axis=0), env[1]

    def act_major(item, env, down=True):
        acted = dot(env[0], wq[item])
        acted = swap_groups(join_lanes(join_rows(acted)) * env[1])
        if down:
            keep(item, acted)
        return rows_to_lanes(acted)

    def close(left, right):
        high, low = halves(right)
        wide = jnp.concatenate([high] * rep + [low] * rep, axis=0)
        tall = jnp.concatenate(halves(left), axis=0)
        return scaled(join_lanes(join_rows(dot_nt(tall, wide))))

    def mix(item, state):
        state, scale = state
        pair = stacked(state)
        parts = jnp.concatenate([pair, pair], axis=1)
        return lanes_to_rows(join_rows(dot(parts, wm[item])) * scale)

    def settle(square):
        square = join_lanes(join_rows(square))
        total = square[:chi]
        for i in range(1, rep):
            total = jnp.where(group == i, square[i * chi : (i + 1) * chi], total)
        return scaled(total, unfolded_mask)

    def descend(items, mixes):
        squares = [
            dot(yt[item], jnp.concatenate(halves(mixed), axis=1))
            for item, mixed in zip(items, mixes, strict=True)
        ]
        return [settle(square) for square in squares]

    envs = [[(unflatten(leaf_ref[0, n : n + 1, :]), 1.0) for n in range(leaves)]]
    early = leaves >> 1
    for move in local_moves[:early]:
        move.forward()
    for move in group_moves:
        move.wait_recv()
    if joint < levels:
        far_copy(joint)
    top_spread(0)
    for move in local_moves[early:]:
        move.forward()

    late = []
    first = 0
    for height in range(1, height_dev + 1):
        current = envs[-1]
        count = leaves >> height
        majors = [for_major(current[2 * n]) for n in range(count)]
        minors = [for_minor(current[2 * n + 1]) for n in range(count)]
        for n in range(count):
            local_moves[first + n].finish()
        for n in range(count):
            node = first + n
            store_up(2 * node, jnp.concatenate([loc[j, node] for j in range(bonds)], axis=0))
        lefts = [act_major(2 * (first + n), majors[n], False) for n in range(count)]
        rights = [act_minor(2 * (first + n), minors[n]) for n in range(count)]
        late.extend(zip(lefts, rights, strict=True))
        grown = [close(lefts[n], rights[n]) for n in range(count)]
        envs.append(grown)
        first += count

    env = envs[-1][0]

    def env_copy(slot, n, hop):
        copy = pltpu.make_async_remote_copy(
            src_ref=esend.at[slot],
            dst_ref=erecv.at[n],
            send_sem=env_send.at[n],
            recv_sem=env_recv.at[n],
            device_id=(position ^ hop, mine),
            device_id_type=MESH,
        )
        copy.start()
        sends.append(copy)
        return copy

    def assemble(base, count, start, width):
        rows = []
        for j in range(bonds):
            rows.append(
                jnp.concatenate(
                    [raw[j, base + s, :, start : start + width] for s in range(count)], axis=1
                )
            )
        return jnp.concatenate(rows, axis=0)

    def top_value(k, r=0):
        base = ((position ^ r) >> (k + 1)) << (k + 1)
        return assemble(base, 2 << k, starts[k], cols >> (k + 1))

    def is_upper(k):
        return lax.rem(position >> k, 2) == 1

    def own_nodes(ks):
        values = [top_value(k) for k in ks]
        moved = permute([stacked(value) for value in values])
        for n, k in enumerate(ks):
            chosen = jnp.where(is_upper(k), values[n], moved[n])
            store_up(2 * nodes + k, chosen)
            store_down(2 * nodes + k, chosen)

    def local_values():
        return [
            jnp.concatenate([loc[j, node] for j in range(bonds)], axis=0) for node in range(nodes)
        ]

    esend[0] = packed(env[0])
    group_envs = [env_copy(0, hop - 1, hop) for hop in reversed(range(1, span))]

    top_moves[0].forward()
    locals_ = local_values()
    more = permute([stacked(value) for value in locals_] + [stacked(right) for _, right in late])
    for node in range(nodes):
        store_down(2 * node, locals_[node])
        store_down(2 * node + 1, more[node])
        keep(2 * node, lanes_to_rows(late[node][0]))
        keep(2 * node + 1, lanes_to_rows(more[nodes + node]))
    if joint < levels:
        far_moves[0].wait_recv()
        if joint + 1 < levels:
            far_copy(joint + 1)
        top_spread(joint)
    top_moves[0].finish()

    extra = 2 * nodes + levels
    others = {}
    tops = [top_value(k) for k in range(joint)]
    for k in range(joint):
        store_up(2 * nodes + k, tops[k])
        others[k, 0] = 2 * nodes + k
        for r in range(2 << k, span, 2 << k):
            store_up(extra, top_value(k, r))
            others[k, r] = extra
            extra += 1
    for copy in group_envs:
        copy.wait_recv()
    pool = {0: env}
    for hop in range(1, span):
        pool[hop] = scaled(unpacked(erecv[hop - 1]))
    acted = []
    for k in range(joint):
        up = is_upper(k)
        sides = {}
        for r in range(0, span, 2 << k):
            near, far = pool[r], pool[r ^ (1 << k)]
            left = [jnp.where(up, x, y) for x, y in zip(far, near, strict=True)]
            right = [jnp.where(up, x, y) for x, y in zip(near, far, strict=True)]
            sides[r] = for_major(left), for_minor(right)
        lefts = {r: act_major(others[k, r], side[0], False) for r, side in sides.items()}
        rights = {r: act_minor(others[k, r], side[1]) for r, side in sides.items()}
        following = {r: close(lefts[r], rights[r]) for r in sides}
        acted.append((lefts[0], rights[0]))
        pool = following
    env = pool[0]

    for k in range(joint, levels):
        esend[1 + k - joint] = packed(env[0])
        copy = env_copy(1 + k - joint, span - 1 + k - joint, 1 << k)
        index = k - joint + 1
        top_moves[index].forward()
        if k == joint:
            moved = permute(
                [stacked(value) for value in tops] + [stacked(right) for _, right in acted]
            )
            for n in range(joint):
                up = is_upper(n)
                store_down(2 * nodes + n, jnp.where(up, tops[n], moved[n]))
                chosen = jnp.where(up, acted[n][0], moved[joint + n])
                keep(2 * nodes + n, lanes_to_rows(chosen))
        if k + 1 < levels:
            far_moves[index].wait_recv()
            if k + 2 < levels:
                far_copy(k + 2)
            top_spread(k + 1)
        top_moves[index].finish()
        own_nodes([k])
        item = 2 * nodes + k
        minor = act_minor(item, for_minor(env))
        if k == levels - 1:
            root = assemble(0, devices, starts[levels], cols >> levels)
            state = close(root, root)
            state = jnp.where(group == 0, state[0], 0.0), state[1]
            keep(item, mix(item, state))
        copy.wait_recv()
        last = k == levels - 1
        major = act_major(item, for_major(scaled(unpacked(erecv[span - 1 + k - joint]))), not last)
        env = close(major, minor)
    if joint == levels:
        root = assemble(0, devices, starts[levels], cols >> levels)
        state = close(root, root)
        mixed = mix(2 * nodes + levels - 1, state)

    top = jnp.where(group == 0, env[0], 0.0), env[1]
    for k in range(levels - 1, -1, -1):
        marked = lax.rem(position + 1, 2 << k) == 1 << k
        top = [jnp.where(marked, x, y) for x, y in zip(state, top, strict=True)]
        mixed = lanes_to_rows(major) if k == levels - 1 else mix(2 * nodes + k, state)
        (state,) = descend([2 * nodes + k], [mixed])
    out[leaves + nodes] = normal(top)
    states = [state]
    for height in range(height_dev, 0, -1):
        count = leaves >> height
        offset = leaves - 2 * count
        for n in range(count):
            out[leaves + offset + n] = normal(states[n])
        items = [2 * (offset + n) + 1 - side for n in range(count) for side in range(2)]
        states = descend(items, [mix(item, states[n // 2]) for n, item in enumerate(items)])
    for n in range(leaves):
        out[n] = normal(states[n])
    for copy in sends:
        copy.wait_send()


def place(leaves, nodes, packed, leaf_out, inner_out, top_out):
    chi = packed.shape[1]
    rep = LANES // chi
    row = lax.broadcasted_iota(jnp.int32, (SUBLANES, LANES), 0)
    row_mask = lax.broadcasted_iota(jnp.int32, (SUBLANES, LANES), 1) // chi == lax.rem(row, rep)
    first = 0
    for ref, count in ((leaf_out, leaves), (inner_out, nodes), (top_out, 1)):
        for n in range(count):
            for v in range(0, chi, SUBLANES):
                value = jnp.where(row_mask, packed[first + n, v : v + SUBLANES], 0.0)
                step = 1
                while step < rep:
                    value = value + pltpu.roll(value, SUBLANES - step, 0)
                    step *= 2
                for r in range(0, SUBLANES, rep):
                    g = (v + r) // rep
                    spot = (n, slice(0, 1)) if ref is inner_out else (0, slice(n, n + 1))
                    ref[spot + (slice(g * LANES, (g + 1) * LANES),)] = value[r : r + 1]
        first += count


def body(cfg, leaf_metric, local_iso, top_iso):
    chi, leaves, devices, bonds = cfg
    cols = chi * chi
    nodes = leaves - 1
    levels = devices.bit_length() - 1
    joint = min(JOINT, levels)
    span = 1 << joint
    share = chi // bonds
    items = 2 * nodes + levels + span - 1 - joint
    moves = levels - joint + 1
    f32 = jnp.float32
    dma = pltpu.SemaphoreType.DMA
    vmem = pl.BlockSpec(memory_space=pltpu.VMEM)
    hbm = pl.BlockSpec(memory_space=pl.ANY)
    packed = pl.pallas_call(
        functools.partial(kernel, cfg),
        out_shape=pltpu.VMEM((leaves + nodes + 1, chi, LANES), f32),
        in_specs=[hbm] * 3,
        out_specs=vmem,
        scratch_shapes=[
            pltpu.VMEM((1, leaves, cols), f32),
            pltpu.VMEM((bonds, devices, share, cols), f32),
            pltpu.VMEM((bonds, nodes, share, cols), f32),
            pltpu.VMEM((items, cols * chi // LANES, 2 * LANES), jnp.bfloat16),
            pltpu.VMEM((items, 2 * LANES, cols), jnp.bfloat16),
            pltpu.VMEM((items, cols * chi // LANES, 2 * LANES), jnp.bfloat16),
            pltpu.VMEM((items, 2 * LANES, cols * chi // LANES), jnp.bfloat16),
            pltpu.VMEM((4, chi, cols * chi // LANES), f32),
            pltpu.VMEM((cols, cols), jnp.bfloat16),
            pltpu.VMEM((moves, chi * chi // LANES, LANES), f32),
            pltpu.VMEM((span - 2 + moves, chi * chi // LANES, LANES), f32),
            dma((3,)),
            dma((nodes, bonds - 1)),
            dma((nodes, bonds - 1)),
            dma((span - 2 + moves,)),
            dma((span - 2 + moves,)),
            dma((moves, bonds - 1)),
            dma((moves, bonds - 1)),
            dma((span - 2 + moves,)),
            dma((span - 2 + moves,)),
        ],
        compiler_params=pltpu.CompilerParams(collective_id=0, has_side_effects=True),
        name="tree_sweep",
    )(leaf_metric, local_iso, top_iso)
    shapes = ((1, leaves, cols), (nodes, 1, cols), (1, 1, cols))
    leaf_rho, inner_rho, top_rho = pl.pallas_call(
        functools.partial(place, leaves, nodes),
        out_shape=tuple(jax.ShapeDtypeStruct(shape, f32) for shape in shapes),
        in_specs=[vmem],
        out_specs=(vmem,) * 3,
        name="place",
    )(pltpu.with_memory_space_constraint(packed, pltpu.VMEM))
    return leaf_rho, inner_rho.transpose(1, 0, 2), top_rho


def solution(mesh):
    devices, bonds = mesh.shape["leaf"], mesh.shape["bond"]
    spec = P("bond", "leaf", None)
    iso = P("leaf", "bond", None)

    def whole(leaf_metric, local_iso, top_iso):
        cfg = (local_iso.shape[1], leaf_metric.shape[1] // devices, devices, bonds)
        return jax.shard_map(
            functools.partial(body, cfg),
            mesh=mesh,
            in_specs=(spec, iso, iso),
            out_specs=(spec, spec, spec),
            check_vma=False,
        )(leaf_metric, local_iso, top_iso)

    return whole
```
